32 devices in a mesh: grp: 2 (over y), row: 4 (over x, core), col: 4 (over z).
Axes of the slice: x: 2, y: 2, z: 4, core: 2. Of those that a mesh axis runs over, the one named last changes fastest.
Arguments:
- amplitudes: bfloat16 [32768, 16384], P(('grp', 'row'), 'col'), parts along dimension 0, may hold values from -0.046875 to 0.046875
- cholesky: bfloat16 [1024, 32768], P('row', ('grp', 'col')), parts along dimension 1, may hold values from -1.078125 to 1.078125
- occ_index: int32 [32768], P('grp'), parts along dimension 0, may hold values from 0 to 31
- vir_index: int32 [32768], P('grp'), parts along dimension 0, may hold values from 0 to 511
- eps_occ: float32 [64], P('grp'), parts along dimension 0, may hold values from -2 to -0.3
- eps_vir: float32 [1024], P('grp'), parts along dimension 0, may hold values from 0.2 to 3
Outputs:
- new_amplitudes: bfloat16 [32768, 16384], P(('grp', 'row'), 'col'), parts along dimension 0
The draws below stay inside these ranges and needn't reach their ends.
There are 2 independent parts, one for each index of `grp`. The reference program is written for one: setup_inputs(seed, part) draws one part's arguments, and reference() takes and returns one part's arrays. A program takes and returns all parts, laid end to end along the dimension named above; each array names one. Nothing has to cross between parts.
All inputs are finite; a program needn't handle non-finite values.
Results may differ from the reference program's by a relative error of at most 0.0056.
Values may be sent and summed in bfloat16 or wider, within the bound.
A program may use at most 128 MiB of HBM per device.

```python
import math
import jax
import jax.numpy as jnp
from jax import lax

NOCC = 32
NVIR = 512
NAUX = 1024
P_SIZE = 16384


def place_ends(drawn, own_key, least, largest):
    dims = drawn.shape
    index_at = [jax.random.randint(jax.random.fold_in(own_key, axis), (), 0, dims[axis]) for axis in range(len(dims))]
    drawn = drawn.at[tuple(index_at)].set(least)
    longest = dims.index(max(dims))
    index_at[longest] = (index_at[longest] + 1) % dims[longest]
    return drawn.at[tuple(index_at)].set(largest)


def steps_of(stream_key, shape, pieces, least, top_value):
    factor_of, own = 1.0, jax.random.fold_in(stream_key, 6)
    for axis_at, parts in pieces:
        heights = jnp.exp(jax.random.uniform(jax.random.fold_in(own, axis_at), (parts,), jnp.float32, least / len(pieces), top_value / len(pieces)))
        factor_of = factor_of * jnp.repeat(heights, shape[axis_at] // parts).reshape([-1 if axis == axis_at else 1 for axis in range(len(shape))])
    return factor_of


def gaussian(rng, extent, scale, limit, shards=(), kind=jnp.bfloat16):
    entries = scale * jax.random.normal(rng, extent, jnp.float32)
    if shards:
        entries = entries * steps_of(rng, extent, shards, -0.22, 0.18)
    return jnp.clip(entries, -limit, limit).astype(kind)


def setup_inputs(seed: int = 0, part: int = 0) -> dict:
    splits = jax.random.split(jax.random.key(seed), 7)
    part_splits = jax.random.split(jax.random.fold_in(splits[6], part), 7)
    return {
        "amplitudes": gaussian(part_splits[0], (P_SIZE, P_SIZE), P_SIZE ** -0.5, 0.046875, ((0, 4), (1, 4))),
        "cholesky": gaussian(part_splits[1], (NAUX, P_SIZE), 0.18, 1.078125, ((0, 4), (1, 4))),
        "occ_index": place_ends(jax.random.randint(part_splits[2], (P_SIZE,), 0, NOCC), jax.random.fold_in(part_splits[2], 1), 0, NOCC - 1).astype(jnp.int32),
        "vir_index": place_ends(jax.random.randint(part_splits[3], (P_SIZE,), 0, NVIR), jax.random.fold_in(part_splits[3], 1), 0, NVIR - 1).astype(jnp.int32),
        "eps_occ": jnp.clip(jax.random.uniform(part_splits[4], (NOCC,), jnp.float32, -2.0, -0.3), -2.0, -0.3),
        "eps_vir": jnp.clip(jax.random.uniform(part_splits[5], (NVIR,), jnp.float32, 0.2, 3.0), 0.2, 3.0),
    }


def reference(amplitudes, cholesky, occ_index, vir_index, eps_occ, eps_vir):
    gap = eps_vir[vir_index] - eps_occ[occ_index]
    dressed = jnp.dot(cholesky, amplitudes, preferred_element_type=jnp.float32)
    ydress = (cholesky.astype(jnp.float32) + dressed).astype(jnp.bfloat16)
    width = math.gcd(P_SIZE, 1024)

    def gram_block(block_id):
        columns = lax.dynamic_slice_in_dim(ydress, block_id * width, width, 1)
        gram = lax.dot_general(columns, ydress, (((0,), (0,)), ((), ())), preferred_element_type=jnp.float32)
        gaps = lax.dynamic_slice_in_dim(gap, block_id * width, width, 0)
        return (-gram / (gaps[:, None] + gap[None, :])).astype(jnp.bfloat16)

    blocks = lax.map(gram_block, jnp.arange(P_SIZE // width, dtype=jnp.int32))
    return blocks.reshape(P_SIZE, P_SIZE)
```

```python
import functools

import jax
import jax.numpy as jnp
from jax import lax
from jax.experimental import pallas as pl
from jax.experimental.pallas import tpu as pltpu
from jax.sharding import PartitionSpec as P

MESH = pl.DeviceIdType.MESH


def pair_gaps(occ_index, vir_index, eps_occ, eps_vir, begin_pair, pair_count):
    occ_rows = lax.dynamic_slice_in_dim(occ_index, begin_pair, pair_count, 0)
    vir_rows = lax.dynamic_slice_in_dim(vir_index, begin_pair, pair_count, 0)
    occ_table = jnp.arange(eps_occ.shape[0], dtype=jnp.int32)
    vir_table = jnp.arange(eps_vir.shape[0], dtype=jnp.int32)
    occ_energy = jnp.sum(
        jnp.where(occ_rows[:, None] == occ_table[None, :], eps_occ[None, :], 0.0), axis=1
    )
    vir_energy = jnp.sum(
        jnp.where(vir_rows[:, None] == vir_table[None, :], eps_vir[None, :], 0.0), axis=1
    )
    return vir_energy - occ_energy


def enter(row_count, col_count, me_row, me_col):
    barrier = pltpu.get_barrier_semaphore()
    for step in range(1, row_count):
        pl.semaphore_signal(
            barrier,
            inc=1,
            device_id={"row": lax.rem(me_row + step, row_count)},
            device_id_type=MESH,
        )
    for condition, where in ((me_col > 0, -1), (me_col < col_count - 1, 1)):

        @pl.when(condition)
        def _():
            pl.semaphore_signal(
                barrier, inc=1, device_id={"col": me_col + where}, device_id_type=MESH
            )

    neighbours = jnp.minimum(me_col, 1) + jnp.minimum(col_count - 1 - me_col, 1)
    pl.semaphore_wait(barrier, row_count - 1 + neighbours)


class Gather:
    def __init__(self, row_count, col_count, pieces, own, rows, held, sems):
        self.row_count, self.col_count, self.pieces = row_count, col_count, pieces
        self.own, self.rows, self.held = own, rows, held
        self.send_line, self.recv_line, self.send_row, self.recv_row, self.keep = sems
        self.me_row, self.me_col = lax.axis_index("row"), lax.axis_index("col")
        self.depth = own.shape[0] // pieces
        self.share = row_count // col_count
        self.width = own.shape[1] // self.share

    def part(self, piece):
        return pl.ds(piece * self.depth, self.depth)

    def block_ref(self, block, piece, mine):
        if mine:
            return self.own.at[self.part(piece), :]
        return self.held.at[block, self.part(piece), :]

    def block_part(self, block, index, piece, mine):
        columns = pl.ds(index * self.width, self.width)
        if mine:
            return self.own.at[self.part(piece), columns]
        return self.held.at[block, self.part(piece), columns]

    def row_ref(self, owner, target, piece):
        half = self.row_count // 2
        other = lax.rem(owner + target, 2)
        base = target + other * (1 - 2 * lax.rem(target, 2))
        slot = lax.rem(owner - base + self.row_count, self.row_count) // 2 + other * half
        begin = pl.multiple_of(slot * self.depth, self.depth)
        return self.rows.at[piece, pl.ds(begin, self.depth), :]

    def line_copy(self, side, block, hops, piece):
        return pltpu.make_async_remote_copy(
            src_ref=self.block_ref(block, piece, hops == 0),
            dst_ref=self.held.at[block, self.part(piece), :],
            send_sem=self.send_line.at[side, hops, piece],
            recv_sem=self.recv_line.at[side, hops, piece],
            device_id={"col": self.me_col + (1 if side == 0 else -1)},
            device_id_type=MESH,
        )

    def row_copy(self, block, index, piece, mine=False):
        return pltpu.make_async_remote_copy(
            src_ref=self.block_part(block, index, piece, mine),
            dst_ref=self.row_ref(self.me_row, block * self.share + index, piece),
            send_sem=self.send_row.at[block, index, piece],
            recv_sem=self.recv_row.at[self.me_row, piece],
            device_id={"row": block * self.share + index},
            device_id_type=MESH,
        )

    def keep_copy(self, block, index, piece, mine=False):
        return pltpu.make_async_copy(
            self.block_part(block, index, piece, mine),
            self.row_ref(self.me_row, self.me_row, piece),
            self.keep.at[piece],
        )

    def on(self, side):
        return self.me_col < self.col_count - 1 if side == 0 else self.me_col > 0

    def spread(self, block, piece, mine=False):
        for index in range(self.share):
            target = block * self.share + index

            @pl.when(target == self.me_row)
            def _():
                self.keep_copy(block, index, piece, mine).start()

            @pl.when(target != self.me_row)
            def _():
                self.row_copy(block, index, piece, mine).start()

    def begin(self, piece):
        for side in range(2):

            @pl.when(self.on(side))
            def _():
                self.line_copy(side, self.me_col, 0, piece).start()

        self.spread(self.me_col, piece, True)

    def source(self, side, hops):
        block = self.me_col - hops if side == 0 else self.me_col + hops
        exists = self.me_col >= hops if side == 0 else self.me_col + hops < self.col_count
        return block, exists

    def arrive(self, hops, piece):
        for side in range(2):
            block, exists = self.source(side, hops)

            @pl.when(exists)
            def _():
                self.line_copy(side, block, hops - 1, piece).wait_recv()

                if hops < self.col_count - 1:

                    @pl.when(self.on(side))
                    def _():
                        self.line_copy(side, block, hops, piece).start()

                self.spread(block, piece)

    def wait_rows(self, piece):
        for other in range(self.row_count):

            @pl.when(other != self.me_row)
            def _():
                pltpu.make_async_remote_copy(
                    src_ref=self.row_ref(other, self.me_row, piece),
                    dst_ref=self.row_ref(other, self.me_row, piece),
                    send_sem=self.send_row.at[0, 0, piece],
                    recv_sem=self.recv_row.at[other, piece],
                    device_id={"row": other},
                    device_id_type=MESH,
                ).wait_recv()

        for block in range(self.col_count):
            for index in range(self.share):

                @pl.when(block * self.share + index == self.me_row)
                def _():
                    self.keep_copy(block, index, piece).wait()

    def wait_sends(self, piece):
        for side in range(2):
            for hops in range(self.col_count - 1):
                block, exists = self.source(side, hops)

                @pl.when(jnp.logical_and(exists, self.on(side)))
                def _():
                    self.line_copy(side, block, hops, piece).wait_send()

        for block in range(self.col_count):
            for index in range(self.share):

                @pl.when(block * self.share + index != self.me_row)
                def _():
                    self.row_copy(block, index, piece).wait_send()


def gather_sems(row_count, col_count, pieces):
    return [
        pltpu.SemaphoreType.DMA((2, col_count, pieces)),
        pltpu.SemaphoreType.DMA((2, col_count, pieces)),
        pltpu.SemaphoreType.DMA((col_count, row_count // col_count, pieces)),
        pltpu.SemaphoreType.DMA((row_count, pieces)),
        pltpu.SemaphoreType.DMA((pieces,)),
    ]


class Columns:
    def __init__(self, row_count, pieces, own, cols, sems):
        self.row_count, self.pieces, self.own, self.cols = row_count, pieces, own, cols
        self.load, self.send, self.recv, self.send_on = sems
        self.me_row = lax.axis_index("row")
        self.partner = self.me_row + 1 - 2 * lax.rem(self.me_row, 2)
        self.depth = own.shape[0] // pieces

    def part(self, piece):
        return pl.ds(piece * self.depth, self.depth)

    def copy(self, owner, target, sem, piece, src=None):
        dst = self.cols.at[owner, self.part(piece), :]
        return pltpu.make_async_remote_copy(
            src_ref=dst if src is None else src,
            dst_ref=dst,
            send_sem=sem,
            recv_sem=self.recv.at[owner, piece],
            device_id={"row": target},
            device_id_type=MESH,
        )

    def peers(self):
        peers = [(0, self.partner)]
        for step in range(1, self.row_count // 2):
            peers.append((step, lax.rem(self.me_row + 2 * step, self.row_count)))
        return peers

    def first(self, slot, target, piece, src):
        return self.copy(self.me_row, target, self.send.at[slot, piece], piece, src)

    def begin(self, piece, src):
        for slot, target in self.peers():
            self.first(slot, target, piece, src).start()

    def arrive(self, piece):
        for slot, owner in self.peers()[1:]:
            self.copy(owner, self.partner, self.send_on.at[slot, piece], piece).wait_recv()
            self.copy(owner, self.partner, self.send_on.at[slot, piece], piece).start()

    def finish(self, piece, src):
        for slot, target in self.peers():
            self.first(slot, target, piece, src).wait_send()
        self.copy(self.partner, self.partner, self.send.at[0, piece], piece).wait_recv()
        for slot, owner in self.peers()[1:]:
            self.copy(owner, self.partner, self.send_on.at[slot, piece], piece).wait_send()
            theirs = lax.rem(self.partner + 2 * slot, self.row_count)
            self.copy(theirs, self.partner, self.send.at[0, piece], piece).wait_recv()


def columns_sems(row_count, pieces):
    return [
        pltpu.SemaphoreType.DMA((pieces,)),
        pltpu.SemaphoreType.DMA((row_count // 2, pieces)),
        pltpu.SemaphoreType.DMA((row_count, pieces)),
        pltpu.SemaphoreType.DMA((row_count // 2, pieces)),
    ]


class Chunks:
    def __init__(self, row_count, col_count, chunks, own, rows, held, sems):
        self.row_count, self.col_count, self.chunks = row_count, col_count, chunks
        self.own, self.rows, self.held = own, rows, held
        self.send_line, self.recv_line, self.send_row, self.recv_row, self.keep = sems
        self.me_row, self.me_col = lax.axis_index("row"), lax.axis_index("col")
        self.share = row_count // col_count
        self.pieces = chunks * self.share
        self.depth = own.shape[0]
        self.width = own.shape[1] // self.pieces

    def block_ref(self, block, chunk, index, mine):
        if mine:
            begin = pl.multiple_of((index * self.chunks + chunk) * self.width, self.width)
            return self.own.at[:, pl.ds(begin, self.width)]
        return self.held.at[block, chunk * self.share + index]

    def row_ref(self, owner, chunk):
        begin = pl.multiple_of(owner * self.depth, self.depth)
        return self.rows.at[chunk, pl.ds(begin, self.depth), :]

    def line_copy(self, side, block, hops, chunk, index, mine=False):
        piece = chunk * self.share + index
        return pltpu.make_async_remote_copy(
            src_ref=self.block_ref(block, chunk, index, mine),
            dst_ref=self.held.at[block, piece],
            send_sem=self.send_line.at[side, hops, piece],
            recv_sem=self.recv_line.at[side, hops, piece],
            device_id={"col": self.me_col + (1 if side == 0 else -1)},
            device_id_type=MESH,
        )

    def row_copy(self, block, chunk, index, mine=False):
        return pltpu.make_async_remote_copy(
            src_ref=self.block_ref(block, chunk, index, mine),
            dst_ref=self.row_ref(self.me_row, chunk),
            send_sem=self.send_row.at[block, chunk * self.share + index],
            recv_sem=self.recv_row.at[self.me_row, chunk],
            device_id={"row": block * self.share + index},
            device_id_type=MESH,
        )

    def keep_copy(self, block, chunk, index, mine=False):
        return pltpu.make_async_copy(
            self.block_ref(block, chunk, index, mine),
            self.row_ref(self.me_row, chunk),
            self.keep.at[chunk],
        )

    def on(self, side):
        return self.me_col < self.col_count - 1 if side == 0 else self.me_col > 0

    def spread(self, block, chunk, index, mine=False):
        target = block * self.share + index

        @pl.when(target == self.me_row)
        def _():
            self.keep_copy(block, chunk, index, mine).start()

        @pl.when(target != self.me_row)
        def _():
            self.row_copy(block, chunk, index, mine).start()

    def begin(self, chunk):
        for index in range(self.share):
            for side in range(2):

                @pl.when(self.on(side))
                def _():
                    self.line_copy(side, self.me_col, 0, chunk, index, True).start()

            self.spread(self.me_col, chunk, index, True)

    def source(self, side, hops):
        block = self.me_col - hops if side == 0 else self.me_col + hops
        exists = self.me_col >= hops if side == 0 else self.me_col + hops < self.col_count
        return block, exists

    def arrive(self, hops, chunk):
        for side in range(2):
            block, exists = self.source(side, hops)

            @pl.when(exists)
            def _():
                for index in range(self.share):
                    self.line_copy(side, block, hops - 1, chunk, index).wait_recv()

                    @pl.when(jnp.logical_and(self.on(side), hops < self.col_count - 1))
                    def _():
                        self.line_copy(side, block, hops, chunk, index).start()

                    self.spread(block, chunk, index)

    def wait_rows(self, chunk):
        for other in range(self.row_count):

            @pl.when(other != self.me_row)
            def _():
                pltpu.make_async_remote_copy(
                    src_ref=self.row_ref(other, chunk),
                    dst_ref=self.row_ref(other, chunk),
                    send_sem=self.send_row.at[0, 0],
                    recv_sem=self.recv_row.at[other, chunk],
                    device_id={"row": other},
                    device_id_type=MESH,
                ).wait_recv()

        pltpu.make_async_copy(
            self.row_ref(self.me_row, chunk), self.row_ref(self.me_row, chunk), self.keep.at[chunk]
        ).wait()

    def wait_sends(self, chunk):
        for index in range(self.share):
            for side in range(2):
                for hops in range(self.col_count - 1):
                    block, exists = self.source(side, hops)

                    @pl.when(jnp.logical_and(exists, self.on(side)))
                    def _():
                        self.line_copy(side, self.me_col, hops, chunk, index).wait_send()

            for block in range(self.col_count):

                @pl.when(block * self.share + index != self.me_row)
                def _():
                    self.row_copy(block, chunk, index).wait_send()


def chunk_sems(row_count, col_count, chunks):
    pieces = chunks * (row_count // col_count)
    return [
        pltpu.SemaphoreType.DMA((2, col_count, pieces)),
        pltpu.SemaphoreType.DMA((2, col_count, pieces)),
        pltpu.SemaphoreType.DMA((col_count, pieces)),
        pltpu.SemaphoreType.DMA((row_count, chunks)),
        pltpu.SemaphoreType.DMA((chunks,)),
    ]


def turn(chunk_ref, turned, gap_rows, gap_turned, begin):
    rows = turned.shape[0]
    turned[...] = chunk_ref[...].T
    gaps = gap_rows[:, pl.ds(pl.multiple_of(begin, rows), rows)]
    gap_turned[...] = jnp.broadcast_to(gaps, (128, rows)).T


def quotient(turned, right, gap_turned, gap_cols, span):
    gram = jnp.dot(turned[...], right, preferred_element_type=jnp.float32)
    copies = gram.shape[1] // 128
    total = jnp.concatenate([gap_turned[...]] * copies, axis=1) + gap_cols[:, span]
    return (-gram / total).astype(jnp.bfloat16)


def dress_kernel(
    row_count, col_count, pieces, chunks, ready, amplitudes, own, gap_rows, gap_cols,
    held, held_y, y_rows, y_cols, done, dressed, table, rows, mine, kept,
    to_partner, from_partner, to_peer, from_peer, chol, chunk_buf, turned, gap_turned, staged,
    table_sem, chol_sem, partner_send, partner_recv, peer_send, peer_recv,
    right_sem, chunk_sem, staged_sem, *sems
):
    gather = Gather(row_count, col_count, pieces, own, rows, held, sems[:5])
    second = Chunks(row_count, col_count, chunks, dressed, y_rows, held_y, sems[5:10])
    columns = Columns(row_count, pieces, dressed, y_cols, sems[10:])
    me_row, depth = gather.me_row, gather.depth
    partner = me_row + 1 - 2 * lax.rem(me_row, 2)
    half = row_count // 2
    split = table_sem.shape[0]
    chunk = table.shape[0] // split
    tile = min(512, table.shape[1])
    tiles = table.shape[1] // tile

    def table_copy(index):
        span = pl.ds(index * chunk, chunk)
        return pltpu.make_async_copy(
            amplitudes.at[span, :], table.at[span, :], table_sem.at[index]
        )

    def chol_copy(piece):
        return pltpu.make_async_copy(
            own.at[gather.part(piece), :], chol.at[piece], chol_sem.at[piece]
        )

    def partner_copy(piece):
        return pltpu.make_async_remote_copy(
            src_ref=to_partner.at[piece % 2],
            dst_ref=from_partner.at[piece],
            send_sem=partner_send.at[piece],
            recv_sem=partner_recv.at[piece],
            device_id={"row": partner},
            device_id_type=MESH,
        )

    def peer_copy(step, piece):
        return pltpu.make_async_remote_copy(
            src_ref=to_peer.at[piece % 2, step - 1],
            dst_ref=from_peer.at[piece, half - step - 1],
            send_sem=peer_send.at[piece, step],
            recv_sem=peer_recv.at[piece, half - step],
            device_id={"row": lax.rem(me_row + 2 * step, row_count)},
            device_id_type=MESH,
        )

    def multiply(piece):
        if piece >= 2:
            partner_copy(piece - 2).wait_send()

        @pl.loop(0, tiles)
        def _(index):
            span = pl.ds(pl.multiple_of(index * tile, tile), tile)
            product = jnp.dot(
                rows[piece], table[:, span], preferred_element_type=jnp.float32
            )
            mine[:, span] = product[: half * depth]
            to_partner[piece % 2, :, span] = product[half * depth :].astype(jnp.bfloat16)

        partner_copy(piece).start()

    def pair(piece):
        partner_copy(piece).wait_recv()
        if piece >= 2:
            for step in range(1, half):
                peer_copy(step, piece - 2).wait_send()

        @pl.loop(0, tiles)
        def _(index):
            span = pl.ds(pl.multiple_of(index * tile, tile), tile)
            both = mine[:, span] + from_partner[piece, :, span].astype(jnp.float32)
            kept[piece % 2, :, span] = both[:depth]
            for step in range(1, half):
                to_peer[piece % 2, step - 1, :, span] = both[
                    step * depth : (step + 1) * depth
                ].astype(jnp.bfloat16)

        for step in range(1, half):
            peer_copy(step, piece).start()

    def close(piece):
        chol_copy(piece).wait()
        for step in range(1, half):
            peer_copy(step, piece).wait_recv()

        @pl.loop(0, tiles)
        def _(index):
            span = pl.ds(pl.multiple_of(index * tile, tile), tile)
            total = kept[piece % 2, :, span]
            for step in range(1, half):
                total = total + from_peer[piece, step - 1, :, span].astype(jnp.float32)
            total = chol[piece, :, span].astype(jnp.float32) + total
            dressed[gather.part(piece), span] = total.astype(jnp.bfloat16)

    def own_y(piece):
        return dressed.at[gather.part(piece), :]

    def own_cols(piece):
        return pltpu.make_async_copy(
            own_y(piece), y_cols.at[me_row, gather.part(piece), :], columns.load.at[piece]
        )

    full = dressed.shape[0]

    def right_copy(owner):
        return pltpu.make_async_copy(
            y_cols.at[owner], table.at[pl.ds(owner * full, full), :], right_sem.at[owner]
        )

    def chunk_copy(index):
        return pltpu.make_async_copy(y_rows.at[index], chunk_buf, chunk_sem.at[0])

    def staged_copy(index, at):
        slot = lax.rem(at, 2)
        begin = pl.multiple_of(index * second.width, second.width)
        span = pl.ds(pl.multiple_of(at * tile, tile), tile)
        return pltpu.make_async_copy(
            staged.at[slot], done.at[pl.ds(begin, second.width), span], staged_sem.at[slot]
        )

    def divide(index):
        chunk_copy(index).wait()
        turn(chunk_buf, turned, gap_rows, gap_turned, index * second.width)

        @pl.loop(0, tiles)
        def _(at):
            @pl.when(jnp.logical_or(index > 0, at >= 2))
            def _():
                staged_copy(index, at).wait()

            span = pl.ds(pl.multiple_of(at * tile, tile), tile)
            right = table[: row_count * full, span]
            staged[lax.rem(at, 2)] = quotient(turned, right, gap_turned, gap_cols, span)
            staged_copy(index, at).start()

    enter(row_count, col_count, gather.me_row, gather.me_col)
    for piece in range(min(2, pieces)):
        gather.begin(piece)
    for index in range(split):
        table_copy(index).start()
    for piece in range(pieces):
        chol_copy(piece).start()
    for step in range(pieces + col_count):
        if step + 2 < pieces:
            gather.begin(step + 2)
        for hops in range(1, col_count):
            if 0 <= step - hops + 1 < pieces:
                gather.arrive(hops, step - hops + 1)
        piece = step - (col_count - 2)
        if 0 <= piece - 1 < pieces:
            pair(piece - 1)
        if 0 <= piece - 2 < pieces:
            close(piece - 2)
            own_cols(piece - 2).start()
            columns.begin(piece - 2, own_y(piece - 2))
        if 0 <= piece < pieces:
            gather.wait_rows(piece)
            if piece == 0:
                for index in range(split):
                    table_copy(index).wait()
            multiply(piece)
        if 0 <= step - col_count - 1 < pieces:
            columns.arrive(step - col_count - 1)

    @pl.loop(0, chunks)
    def _(index):
        second.begin(index)

    columns.arrive(pieces - 1)
    for piece in range(pieces):
        own_cols(piece).wait()
        columns.finish(piece, own_y(piece))
    for owner in range(row_count):
        right_copy(owner).start()

    turn_at = jnp.maximum(jnp.abs(gather.me_col - me_row // second.share), 1)

    @pl.loop(0, (col_count - 1) * chunks)
    def _(step):
        hops = lax.div(step, chunks) + 1
        index = lax.rem(step, chunks)
        go = jnp.logical_and(hops == turn_at, jnp.logical_and(index > 0, index <= ready))

        @pl.when(go)
        def _():
            second.wait_rows(index - 1)
            chunk_copy(index - 1).start()

        second.arrive(hops, index)

        @pl.when(go)
        def _():
            @pl.when(index == 1)
            def _():
                for owner in range(row_count):
                    right_copy(owner).wait()

            divide(index - 1)

    for at in range(2):
        staged_copy(0, at).wait()
    for piece in range(pieces):
        gather.wait_sends(piece)
        if piece >= pieces - 2:
            partner_copy(piece).wait_send()
            for step in range(1, half):
                peer_copy(step, piece).wait_send()

    for index in range(ready, chunks):
        second.wait_rows(index)

    @pl.loop(0, chunks)
    def _(index):
        second.wait_sends(index)


def finish_kernel(
    row_count, ready, done, y_rows, y_cols, gap_rows, gap_cols, out,
    passed, right, chunk_buf, turned, gap_turned, staged,
    right_sem, chunk_sem, read_sem, write_sem, staged_sem
):
    full = y_cols.shape[1]
    late = chunk_buf.shape[0]
    rows, tile = staged.shape[1:]
    tiles = right.shape[1] // tile
    part = passed.shape[1]

    def right_copy(owner):
        return pltpu.make_async_copy(
            y_cols.at[owner], right.at[pl.ds(owner * full, full), :], right_sem.at[owner]
        )

    def chunk_copy(index):
        return pltpu.make_async_copy(
            y_rows.at[ready + index], chunk_buf.at[index], chunk_sem.at[index]
        )

    def read(index):
        begin = pl.multiple_of(index * part, part)
        return pltpu.make_async_copy(
            done.at[pl.ds(begin, part), :], passed.at[index], read_sem.at[index]
        )

    def write(index):
        begin = pl.multiple_of(index * part, part)
        return pltpu.make_async_copy(
            passed.at[index], out.at[pl.ds(begin, part), :], write_sem.at[index]
        )

    def staged_copy(index, at):
        slot = lax.rem(at, 2)
        span = pl.ds(pl.multiple_of(at * tile, tile), tile)
        return pltpu.make_async_copy(
            staged.at[slot], out.at[pl.ds((ready + index) * rows, rows), span], staged_sem.at[slot]
        )

    for owner in range(row_count):
        right_copy(owner).start()
    for index in range(late):
        chunk_copy(index).start()

    @pl.loop(0, late * tiles)
    def _(index):
        read(index).start()

    for owner in range(row_count):
        right_copy(owner).wait()
    for index in range(late):
        chunk_copy(index).wait()
        turn(chunk_buf.at[index], turned, gap_rows, gap_turned, (ready + index) * rows)

        @pl.loop(0, tiles)
        def _(at):
            read(index * tiles + at).wait()
            write(index * tiles + at).start()

            @pl.when(jnp.logical_or(index > 0, at >= 2))
            def _():
                staged_copy(index, at).wait()

            span = pl.ds(pl.multiple_of(at * tile, tile), tile)
            staged[lax.rem(at, 2)] = quotient(turned, right[:, span], gap_turned, gap_cols, span)
            staged_copy(index, at).start()

    for at in range(2):
        staged_copy(0, at).wait()

    @pl.loop(0, late * tiles)
    def _(index):
        write(index).wait()


def update(amplitudes, own, gap_rows, gap_cols, row_count, col_count, collective_id):
    depth, width = own.shape
    rows_width = amplitudes.shape[0]
    pieces = max(1, min(8, depth // 16))
    chunks = max(2, min(8, rows_width // 128))
    late = max(1, chunks // 4)
    ready = chunks - late
    share = row_count // col_count
    span = rows_width // chunks
    tile = min(512, width)
    depth_piece, half = depth // pieces, row_count // 2
    bf16, f32, dma = jnp.bfloat16, jnp.float32, pltpu.SemaphoreType.DMA
    scratch = [
        pltpu.VMEM((depth, width), bf16),
        pltpu.VMEM(amplitudes.shape, bf16),
        pltpu.VMEM((pieces, row_count * depth_piece, amplitudes.shape[0]), bf16),
        pltpu.VMEM((half * depth_piece, width), f32),
        pltpu.VMEM((2, depth_piece, width), f32),
        pltpu.VMEM((2, half * depth_piece, width), bf16),
        pltpu.VMEM((pieces, half * depth_piece, width), bf16),
        pltpu.VMEM((2, half - 1, depth_piece, width), bf16),
        pltpu.VMEM((pieces, half - 1, depth_piece, width), bf16),
        pltpu.VMEM((pieces, depth_piece, width), bf16),
        pltpu.VMEM((row_count * depth, span), bf16),
        pltpu.VMEM((span, row_count * depth), bf16),
        pltpu.VMEM((span, 128), f32),
        pltpu.VMEM((2, span, tile), bf16),
        dma((4,)),
        dma((pieces,)),
        dma((pieces,)),
        dma((pieces,)),
        dma((pieces, half)),
        dma((pieces, half)),
        dma((row_count,)),
        dma((1,)),
        dma((2,)),
    ]
    scratch += gather_sems(row_count, col_count, pieces)
    scratch += chunk_sems(row_count, col_count, chunks) + columns_sems(row_count, pieces)
    anywhere = pl.BlockSpec(memory_space=pl.ANY)
    near = pl.BlockSpec(memory_space=pltpu.VMEM)
    _, _, y_rows, y_cols, done = pl.pallas_call(
        functools.partial(dress_kernel, row_count, col_count, pieces, chunks, ready),
        out_shape=(
            jax.ShapeDtypeStruct((col_count, depth, width), bf16),
            jax.ShapeDtypeStruct((col_count, chunks * share, depth, span), bf16),
            jax.ShapeDtypeStruct((chunks, row_count * depth, span), bf16),
            jax.ShapeDtypeStruct((row_count, depth, width), bf16),
            jax.ShapeDtypeStruct((ready * span, width), bf16),
        ),
        in_specs=[anywhere, anywhere, near, near],
        out_specs=(anywhere,) * 5,
        scratch_shapes=scratch,
        compiler_params=pltpu.CompilerParams(
            collective_id=collective_id, has_side_effects=True, vmem_limit_bytes=67043328
        ),
        name="dress",
    )(amplitudes, own, gap_rows, gap_cols)
    moves = late * (width // tile)
    return pl.pallas_call(
        functools.partial(finish_kernel, row_count, ready),
        out_shape=jax.ShapeDtypeStruct(amplitudes.shape, bf16),
        in_specs=[anywhere] * 3 + [near] * 2,
        out_specs=anywhere,
        scratch_shapes=[
            pltpu.VMEM((moves, ready * span // moves, width), bf16),
            pltpu.VMEM((row_count * depth, width), bf16),
            pltpu.VMEM((late, row_count * depth, span), bf16),
            pltpu.VMEM((span, row_count * depth), bf16),
            pltpu.VMEM((span, 128), f32),
            pltpu.VMEM((2, span, tile), bf16),
            dma((row_count,)),
            dma((late,)),
            dma((moves,)),
            dma((moves,)),
            dma((2,)),
        ],
        compiler_params=pltpu.CompilerParams(vmem_limit_bytes=67043328),
        name="finish",
    )(done, y_rows, y_cols, gap_rows, gap_cols)


def local(row_count, col_count, amplitudes, cholesky, occ_index, vir_index, eps_occ, eps_vir):
    row_position = lax.axis_index("row")
    col_position = lax.axis_index("col")
    rows_block, cols_block = amplitudes.shape
    gap_rows = pair_gaps(
        occ_index, vir_index, eps_occ, eps_vir, row_position * rows_block, rows_block
    )
    gap_cols = pair_gaps(
        occ_index, vir_index, eps_occ, eps_vir, col_position * cols_block, cols_block
    )
    return update(
        amplitudes, cholesky, gap_rows[None, :], gap_cols[None, :], row_count, col_count, 0
    )


def solution(mesh):
    return jax.shard_map(
        functools.partial(local, mesh.shape["row"], mesh.shape["col"]),
        mesh=mesh,
        in_specs=(
            P(("grp", "row"), "col"),
            P("row", ("grp", "col")),
            P("grp"),
            P("grp"),
            P("grp"),
            P("grp"),
        ),
        out_specs=P(("grp", "row"), "col"),
        check_vma=False,
    )
```

```python
import functools

import jax
import jax.numpy as jnp
from jax import lax
from jax.experimental import pallas as pl
from jax.experimental.pallas import tpu as pltpu
from jax.sharding import PartitionSpec as P

MESH = pl.DeviceIdType.MESH
CUTS = 1
CHUNKS = 8
LATE = 2
SPLIT = 2
PLAIN = 4
PLAIN_CHUNKS = 4
LAUNCH_LEAD = 1
BEGIN_LEAD = 2
CLOSE_LAG = 1


def pair_gaps(occ_index, vir_index, eps_occ, eps_vir, begin_pair, pair_count):
    occ_rows = lax.dynamic_slice_in_dim(occ_index, begin_pair, pair_count, 0)
    vir_rows = lax.dynamic_slice_in_dim(vir_index, begin_pair, pair_count, 0)
    occ_table = jnp.arange(eps_occ.shape[0], dtype=jnp.int32)
    vir_table = jnp.arange(eps_vir.shape[0], dtype=jnp.int32)
    occ_energy = jnp.sum(
        jnp.where(occ_rows[:, None] == occ_table[None, :], eps_occ[None, :], 0.0), axis=1
    )
    vir_energy = jnp.sum(
        jnp.where(vir_rows[:, None] == vir_table[None, :], eps_vir[None, :], 0.0), axis=1
    )
    return vir_energy - occ_energy


def enter(row_count, col_count, me_row, me_col):
    barrier = pltpu.get_barrier_semaphore()
    for step in range(1, row_count):
        pl.semaphore_signal(
            barrier,
            inc=1,
            device_id={"row": lax.rem(me_row + step, row_count)},
            device_id_type=MESH,
        )
    for condition, where in ((me_col > 0, -1), (me_col < col_count - 1, 1)):

        @pl.when(condition)
        def _():
            pl.semaphore_signal(
                barrier, inc=1, device_id={"col": me_col + where}, device_id_type=MESH
            )

    neighbours = jnp.minimum(me_col, 1) + jnp.minimum(col_count - 1 - me_col, 1)
    pl.semaphore_wait(barrier, row_count - 1 + neighbours)


class Spread:
    def __init__(self, row_count, col_count, own, rows, held, sems):
        self.row_count, self.col_count = row_count, col_count
        self.own, self.rows, self.held = own, rows, held
        self.send_line, self.recv_line, self.send_row, self.recv_row, self.keep = sems[:5]
        self.send_chain, self.recv_chain = sems[5:]
        self.me_row, self.me_col = lax.axis_index("row"), lax.axis_index("col")
        self.share = row_count // col_count
        home = lax.div(self.me_row, self.share)
        ahead = 1 - 2 * lax.rem(home, 2)
        self.after = self.me_col + ahead
        self.onward = jnp.logical_and(self.after >= 0, self.after < col_count)
        self.distance = (self.me_col - home) * ahead
        self.parts = self.send_chain.shape[1]

    def on(self, side):
        return self.me_col < self.col_count - 1 if side == 0 else self.me_col > 0

    def carried(self, block, side, piece):
        return jnp.logical_or(lax.rem(block + side, 2) == 1, self.plain(piece))

    def source(self, side, hops, piece):
        block = self.me_col - hops if side == 0 else self.me_col + hops
        exists = self.me_col >= hops if side == 0 else self.me_col + hops < self.col_count
        return block, jnp.logical_and(exists, self.carried(block + 2 * hops, side, piece))

    def spread_here(self, block, piece):
        side = jnp.where(block < self.me_col, 0, 1)
        return jnp.logical_or(block == self.me_col, self.carried(block, side, piece))

    def spread(self, block, piece, index, mine=False):
        target = block * self.share + index

        @pl.when(target == self.me_row)
        def _():
            self.keep_copy(block, piece, index, mine).start()

        @pl.when(target != self.me_row)
        def _():
            self.row_copy(block, piece, index, mine).start()

    def begin(self, piece):
        for side in range(2):

            @pl.when(jnp.logical_and(self.on(side), self.carried(self.me_col, side, piece)))
            def _():
                for copy in self.line_copies(side, self.me_col, 0, piece, True):
                    copy.start()

        for index in range(self.share):
            self.spread(self.me_col, piece, index, True)

    def arrive(self, hops, piece):
        for side in range(2):
            block, exists = self.source(side, hops, piece)

            @pl.when(exists)
            def _():
                for copy in self.line_copies(side, block, hops - 1, piece):
                    copy.wait_recv()

                if hops < self.col_count - 1:

                    @pl.when(self.on(side))
                    def _():
                        for copy in self.line_copies(side, block, hops, piece):
                            copy.start()

                for index in range(self.share):
                    self.spread(block, piece, index)

    def line_copies(self, side, block, hops, piece, mine=False):
        return [
            pltpu.make_async_remote_copy(
                src_ref=self.block_ref(block, piece, index, mine),
                dst_ref=self.block_ref(block, piece, index, False),
                send_sem=self.send_line.at[side, hops, piece, index],
                recv_sem=self.recv_line.at[side, hops, piece, index],
                device_id={"col": self.me_col + (1 if side == 0 else -1)},
                device_id_type=MESH,
            )
            for index in range(self.share)
        ]

    def row_copy(self, block, piece, index, mine=False):
        target = block * self.share + index
        return pltpu.make_async_remote_copy(
            src_ref=self.block_ref(block, piece, index, mine),
            dst_ref=self.row_ref(self.me_row, target, piece),
            send_sem=self.send_row.at[block, index, piece],
            recv_sem=self.recv_row.at[self.me_row, piece],
            device_id={"row": target},
            device_id_type=MESH,
        )

    def keep_copy(self, block, piece, index, mine=False):
        return pltpu.make_async_copy(
            self.block_ref(block, piece, index, mine),
            self.row_ref(self.me_row, self.me_row, piece),
            self.keep.at[piece],
        )

    def chain_copy(self, piece, part):
        ref = self.chain_ref(piece, part)
        return pltpu.make_async_remote_copy(
            src_ref=ref,
            dst_ref=ref,
            send_sem=self.send_chain.at[piece, part],
            recv_sem=self.recv_chain.at[piece, part],
            device_id={"col": self.after},
            device_id_type=MESH,
        )

    def wait_rows(self, piece):
        mine = self.row_ref(self.me_row, self.me_row, piece)
        for other in range(self.row_count):

            @pl.when(other != self.me_row)
            def _():
                theirs = self.row_ref(other, self.me_row, piece)
                pltpu.make_async_remote_copy(
                    src_ref=theirs,
                    dst_ref=theirs,
                    send_sem=self.send_row.at[0, 0, piece],
                    recv_sem=self.recv_row.at[other, piece],
                    device_id={"row": other},
                    device_id_type=MESH,
                ).wait_recv()

        pltpu.make_async_copy(mine, mine, self.keep.at[piece]).wait()

    def launch(self, piece):
        @pl.when(self.distance == 0)
        def _():
            self.wait_rows(piece)

            @pl.when(jnp.logical_and(self.onward, jnp.logical_not(self.plain(piece))))
            def _():
                for part in range(self.parts):
                    self.chain_copy(piece, part).start()

    def relay(self, distance, piece):
        @pl.when(jnp.logical_and(self.distance == distance, jnp.logical_not(self.plain(piece))))
        def _():
            for part in range(self.parts):
                self.chain_copy(piece, part).wait_recv()

                @pl.when(self.onward)
                def _():
                    self.chain_copy(piece, part).start()

    def sliced(self, piece):
        plain = jnp.logical_and(self.distance > 0, self.plain(piece))
        return jnp.logical_or(self.distance < 0, plain)

    def settle(self, piece):
        self.relay(self.col_count - 1, piece)

        @pl.when(self.sliced(piece))
        def _():
            self.wait_rows(piece)

    def wait_sends(self, piece):
        for side in range(2):
            for hops in range(self.col_count - 1):
                block, exists = self.source(side, hops, piece)

                @pl.when(jnp.logical_and(exists, self.on(side)))
                def _():
                    for copy in self.line_copies(side, self.me_col, hops, piece):
                        copy.wait_send()

        for block in range(self.col_count):
            for index in range(self.share):

                @pl.when(
                    jnp.logical_and(
                        self.spread_here(block, piece), block * self.share + index != self.me_row
                    )
                )
                def _():
                    self.row_copy(block, piece, index).wait_send()

        chained = jnp.logical_and(self.distance >= 0, jnp.logical_not(self.plain(piece)))

        @pl.when(jnp.logical_and(chained, self.onward))
        def _():
            for part in range(self.parts):
                self.chain_copy(piece, part).wait_send()


class Gather(Spread):
    def __init__(self, row_count, col_count, pieces, cuts, own, rows, held, sems):
        super().__init__(row_count, col_count, own, rows, held, sems)
        self.pieces, self.cuts = pieces, cuts
        self.depth = own.shape[0] // pieces
        self.full = own.shape[1] // self.share
        self.width = self.full // cuts

    def plain(self, unit):
        return unit < self.pieces * self.cuts * PLAIN // 8

    def part(self, piece):
        return pl.ds(pl.multiple_of(piece * self.depth, self.depth), self.depth)

    def span(self, unit, index=0):
        begin = index * self.full + lax.rem(unit, self.cuts) * self.width
        return pl.ds(pl.multiple_of(begin, self.width), self.width)

    def block_ref(self, block, unit, index, mine):
        piece = lax.div(unit, self.cuts)
        if mine:
            return self.own.at[self.part(piece), self.span(unit, index)]
        return self.held.at[block, self.part(piece), self.span(unit, index)]

    def row_ref(self, owner, target, unit):
        half = self.row_count // 2
        other = lax.rem(owner + target, 2)
        base = target + other * (1 - 2 * lax.rem(target, 2))
        slot = lax.div(lax.rem(owner - base + self.row_count, self.row_count), 2) + other * half
        begin = pl.multiple_of(slot * self.depth, self.depth)
        piece = lax.div(unit, self.cuts)
        return self.rows.at[piece, pl.ds(begin, self.depth), self.span(unit)]

    def chain_ref(self, unit, part):
        return self.rows.at[lax.div(unit, self.cuts), :, self.span(unit)]


class Chunks(Spread):
    def __init__(self, row_count, col_count, parts, own, rows, held, sems):
        super().__init__(row_count, col_count, own, rows, held, sems)
        self.chunks = rows.shape[0] // parts
        self.depth = own.shape[0] // parts
        self.width = own.shape[1] // (self.chunks * self.share)

    def plain(self, unit):
        return lax.rem(unit, self.chunks) < self.chunks * PLAIN_CHUNKS // 8

    def block_ref(self, block, unit, index, mine):
        if mine:
            lines = lax.div(unit, self.chunks) * self.depth
            begin = (index * self.chunks + lax.rem(unit, self.chunks)) * self.width
            return self.own.at[
                pl.ds(pl.multiple_of(lines, self.depth), self.depth),
                pl.ds(pl.multiple_of(begin, self.width), self.width),
            ]
        return self.held.at[block, unit, index]

    def row_ref(self, owner, target, unit):
        begin = pl.multiple_of(owner * self.depth, self.depth)
        return self.rows.at[unit, pl.ds(begin, self.depth), :]

    def chain_ref(self, unit, part):
        size = self.rows.shape[1] // self.parts
        return self.rows.at[unit, pl.ds(part * size, size), :]


def spread_sems(row_count, col_count, pieces, parts):
    share = row_count // col_count
    return [
        pltpu.SemaphoreType.DMA((2, col_count, pieces, share)),
        pltpu.SemaphoreType.DMA((2, col_count, pieces, share)),
        pltpu.SemaphoreType.DMA((col_count, share, pieces)),
        pltpu.SemaphoreType.DMA((row_count, pieces)),
        pltpu.SemaphoreType.DMA((pieces,)),
        pltpu.SemaphoreType.DMA((pieces, parts)),
        pltpu.SemaphoreType.DMA((pieces, parts)),
    ]


class Columns:
    def __init__(self, row_count, pieces, own, cols, sems):
        self.row_count, self.pieces, self.own, self.cols = row_count, pieces, own, cols
        self.load, self.send, self.recv, self.send_on = sems
        self.me_row = lax.axis_index("row")
        self.partner = self.me_row + 1 - 2 * lax.rem(self.me_row, 2)
        self.depth = own.shape[0] // pieces

    def part(self, piece):
        return pl.ds(pl.multiple_of(piece * self.depth, self.depth), self.depth)

    def copy(self, owner, target, sem, piece, src=None):
        dst = self.cols.at[owner, self.part(piece), :]
        return pltpu.make_async_remote_copy(
            src_ref=dst if src is None else src,
            dst_ref=dst,
            send_sem=sem,
            recv_sem=self.recv.at[owner, piece],
            device_id={"row": target},
            device_id_type=MESH,
        )

    def peers(self):
        peers = [(0, self.partner)]
        for step in range(1, self.row_count // 2):
            peers.append((step, lax.rem(self.me_row + 2 * step, self.row_count)))
        return peers

    def first(self, slot, target, piece, src):
        return self.copy(self.me_row, target, self.send.at[slot, piece], piece, src)

    def begin(self, piece, src):
        for slot, target in self.peers():
            self.first(slot, target, piece, src).start()

    def arrive(self, piece):
        for slot, owner in self.peers()[1:]:
            self.copy(owner, self.partner, self.send_on.at[slot, piece], piece).wait_recv()
            self.copy(owner, self.partner, self.send_on.at[slot, piece], piece).start()

    def finish(self, piece, src):
        for slot, target in self.peers():
            self.first(slot, target, piece, src).wait_send()
        self.copy(self.partner, self.partner, self.send.at[0, piece], piece).wait_recv()
        for slot, owner in self.peers()[1:]:
            self.copy(owner, self.partner, self.send_on.at[slot, piece], piece).wait_send()
            theirs = lax.rem(self.partner + 2 * slot, self.row_count)
            self.copy(theirs, self.partner, self.send.at[0, piece], piece).wait_recv()


def columns_sems(row_count, pieces):
    return [
        pltpu.SemaphoreType.DMA((pieces,)),
        pltpu.SemaphoreType.DMA((row_count // 2, pieces)),
        pltpu.SemaphoreType.DMA((row_count, pieces)),
        pltpu.SemaphoreType.DMA((row_count // 2, pieces)),
    ]


def right_loads(parts, y_cols, right, sems):
    owners, full, _ = y_cols.shape
    size = full // parts
    return [
        pltpu.make_async_copy(
            y_cols.at[owner, pl.ds(part * size, size), :],
            right.at[pl.ds((part * owners + owner) * size, size), :],
            sems.at[part * owners + owner],
        )
        for part in range(parts)
        for owner in range(owners)
    ]


def chunk_loads(parts, y_rows, index, chunk_ref, sems):
    units, size, _ = y_rows.shape
    return [
        pltpu.make_async_copy(
            y_rows.at[part * (units // parts) + index],
            chunk_ref.at[pl.ds(part * size, size), :],
            sems.at[part],
        )
        for part in range(parts)
    ]


def turn(chunk_ref, turned, gap_rows, gap_turned, begin):
    rows = turned.shape[0]
    turned[...] = chunk_ref[...].T
    gaps = gap_rows[:, pl.ds(pl.multiple_of(begin, rows), rows)]
    gap_turned[...] = jnp.broadcast_to(gaps, (128, rows)).T


def quotient(turned, right, gap_turned, gap_cols, span):
    gram = jnp.dot(turned[...], right, preferred_element_type=jnp.float32)
    copies = gram.shape[1] // 128
    total = jnp.concatenate([gap_turned[...]] * copies, axis=1) + gap_cols[:, span]
    return (-gram / total).astype(jnp.bfloat16)


def dress_kernel(
    row_count, col_count, pieces, cuts, parts, chunks, ready, amplitudes, own, gap_rows, gap_cols,
    held, held_y, y_rows, y_cols, done, dressed, table, rows, mine, kept,
    to_partner, from_partner, to_peer, from_peer, chol, chunk_buf, turned, gap_turned, staged,
    table_sem, chol_sem, partner_send, partner_recv, peer_send, peer_recv,
    right_sem, chunk_sem, staged_sem, *sems
):
    gather = Gather(row_count, col_count, pieces, cuts, own, rows, held, sems[:7])
    full = dressed.shape[0]
    flow = Chunks(row_count, col_count, parts, dressed, y_rows, held_y, sems[7:14])
    columns = Columns(row_count, pieces, dressed, y_cols, sems[14:])
    me_row, depth = gather.me_row, gather.depth
    partner = me_row + 1 - 2 * lax.rem(me_row, 2)
    half = row_count // 2
    split = table_sem.shape[0]
    chunk = table.shape[0] // split
    tile = min(512, table.shape[1])
    tiles = table.shape[1] // tile

    def table_copy(index):
        span = pl.ds(index * chunk, chunk)
        return pltpu.make_async_copy(
            amplitudes.at[span, :], table.at[span, :], table_sem.at[index]
        )

    def chol_copy(piece):
        return pltpu.make_async_copy(
            own.at[gather.part(piece), :], chol.at[piece], chol_sem.at[piece]
        )

    def partner_copy(piece):
        return pltpu.make_async_remote_copy(
            src_ref=to_partner.at[lax.rem(piece, 2)],
            dst_ref=from_partner.at[piece],
            send_sem=partner_send.at[piece],
            recv_sem=partner_recv.at[piece],
            device_id={"row": partner},
            device_id_type=MESH,
        )

    def peer_copy(step, piece):
        return pltpu.make_async_remote_copy(
            src_ref=to_peer.at[lax.rem(piece, 2), step - 1],
            dst_ref=from_peer.at[piece, half - step - 1],
            send_sem=peer_send.at[piece, step],
            recv_sem=peer_recv.at[piece, half - step],
            device_id={"row": lax.rem(me_row + 2 * step, row_count)},
            device_id_type=MESH,
        )

    def multiply(piece, cut):
        @pl.when(jnp.logical_and(cut == 0, piece >= 2))
        def _():
            partner_copy(piece - 2).wait_send()

        @pl.loop(0, tiles // cuts)
        def _(index):
            begin = (cut * (tiles // cuts) + index) * tile
            span = pl.ds(pl.multiple_of(begin, tile), tile)
            product = jnp.dot(
                rows[piece], table[:, span], preferred_element_type=jnp.float32
            )
            mine[:, span] = product[: half * depth]
            to_partner[lax.rem(piece, 2), :, span] = product[half * depth :].astype(jnp.bfloat16)

        @pl.when(cut == cuts - 1)
        def _():
            partner_copy(piece).start()

    def pair(piece):
        partner_copy(piece).wait_recv()

        @pl.when(piece >= 2)
        def _():
            for step in range(1, half):
                peer_copy(step, piece - 2).wait_send()

        @pl.loop(0, tiles)
        def _(index):
            span = pl.ds(pl.multiple_of(index * tile, tile), tile)
            both = mine[:, span] + from_partner[piece, :, span].astype(jnp.float32)
            kept[lax.rem(piece, 2), :, span] = both[:depth]
            for step in range(1, half):
                to_peer[lax.rem(piece, 2), step - 1, :, span] = both[
                    step * depth : (step + 1) * depth
                ].astype(jnp.bfloat16)

        for step in range(1, half):
            peer_copy(step, piece).start()

    def close(piece):
        chol_copy(piece).wait()
        for step in range(1, half):
            peer_copy(step, piece).wait_recv()

        @pl.loop(0, tiles)
        def _(index):
            span = pl.ds(pl.multiple_of(index * tile, tile), tile)
            total = kept[lax.rem(piece, 2), :, span]
            for step in range(1, half):
                total = total + from_peer[piece, step - 1, :, span].astype(jnp.float32)
            total = chol[piece, :, span].astype(jnp.float32) + total
            dressed[gather.part(piece), span] = total.astype(jnp.bfloat16)

    def own_y(piece):
        return dressed.at[gather.part(piece), :]

    def own_cols(piece):
        return pltpu.make_async_copy(
            own_y(piece), y_cols.at[me_row, gather.part(piece), :], columns.load.at[piece]
        )

    def right_copies():
        return right_loads(parts, y_cols, table, right_sem)

    def chunk_copies(index):
        return chunk_loads(parts, y_rows, index, chunk_buf, chunk_sem)

    def staged_copy(index, at):
        slot = lax.rem(at, 2)
        begin = pl.multiple_of(index * flow.width, flow.width)
        span = pl.ds(pl.multiple_of(at * tile, tile), tile)
        return pltpu.make_async_copy(
            staged.at[slot], done.at[pl.ds(begin, flow.width), span], staged_sem.at[slot]
        )

    def divide(index):
        for copy in chunk_copies(index):
            copy.wait()
        turn(chunk_buf, turned, gap_rows, gap_turned, index * flow.width)

        @pl.loop(0, tiles)
        def _(at):
            @pl.when(jnp.logical_or(index > 0, at >= 2))
            def _():
                staged_copy(index, at).wait()

            span = pl.ds(pl.multiple_of(at * tile, tile), tile)
            right = table[: row_count * full, span]
            staged[lax.rem(at, 2)] = quotient(turned, right, gap_turned, gap_cols, span)
            staged_copy(index, at).start()

    enter(row_count, col_count, gather.me_row, gather.me_col)
    units = pieces * cuts
    per = pieces // parts
    rate = chunks // (per * cuts)
    launch_lead = min(LAUNCH_LEAD, units)
    begin_lead = min(BEGIN_LEAD, units)
    pl.loop(0, begin_lead)(gather.begin)
    pl.loop(0, launch_lead)(gather.launch)
    for index in range(split):
        table_copy(index).start()
    for piece in range(pieces):
        chol_copy(piece).start()
    multiply_at = cuts + col_count - 2
    pair_at = multiply_at + cuts
    close_at = pair_at + CLOSE_LAG
    arrive_at = close_at + CLOSE_LAG

    def within(at, count, action):
        @pl.when(jnp.logical_and(at >= 0, at < count))
        def _():
            action(at)

    def every(at, count, action):
        @pl.when(jnp.logical_and(lax.rem(at + 8 * cuts * col_count, cuts) == 0, at >= 0))
        def _():
            within(lax.div(at, cuts), count, action)

    def finish_piece(piece):
        close(piece)
        own_cols(piece).start()
        columns.begin(piece, own_y(piece))

        @pl.when(lax.rem(piece + 1, per) == 0)
        def _():
            begin = lax.div(piece, per) * chunks
            pl.loop(begin, begin + chunks)(flow.begin)

    lag = jnp.maximum(flow.distance * jnp.where(flow.distance < 0, -1, 1), 2) + 1
    flows = parts * chunks
    flow_at = per * cuts + close_at
    last = (parts - 1) * chunks

    def advance(step):
        within(step, flows, flow.launch)
        for hops in range(1, col_count):
            within(step - hops + 1, flows, functools.partial(flow.arrive, hops))
        for distance in range(1, col_count):
            within(step - distance, flows, functools.partial(flow.relay, distance))
        at = step - lag + 1

        @pl.when(jnp.logical_and(flow.sliced(at), jnp.logical_and(at >= 0, at < flows)))
        def _():
            flow.wait_rows(at)

    @pl.loop(0, pieces * cuts + close_at)
    def _(tick):
        within(tick + begin_lead, units, gather.begin)
        within(tick + launch_lead, units, gather.launch)
        for hops in range(1, col_count):
            within(tick - hops + 1, units, functools.partial(gather.arrive, hops))
        for distance in range(1, col_count - 1):
            within(tick - distance, units, functools.partial(gather.relay, distance))
        within(tick - col_count + 1, units, gather.settle)
        every(tick - pair_at, pieces, pair)
        every(tick - close_at, pieces, finish_piece)

        @pl.when(tick == multiply_at)
        def _():
            for index in range(split):
                table_copy(index).wait()

        within(
            tick - multiply_at,
            units,
            lambda at: multiply(lax.div(at, cuts), lax.rem(at, cuts)),
        )
        every(tick - arrive_at, pieces - 1, columns.arrive)

        @pl.when(tick >= flow_at)
        def _():
            begin = (tick - flow_at) * rate
            pl.loop(begin, begin + rate)(advance)

    @pl.loop(last, flows + col_count)
    def _(step):
        at = step - lag - last
        go = jnp.logical_and(at >= 0, at < ready)

        @pl.when(go)
        def _():
            for copy in chunk_copies(at):
                copy.start()

        advance(step)

        @pl.when(step == last + 2)
        def _():
            columns.arrive(pieces - 1)
            for piece in range(pieces):
                own_cols(piece).wait()
                columns.finish(piece, own_y(piece))
            for copy in right_copies():
                copy.start()
            for copy in right_copies():
                copy.wait()

        @pl.when(go)
        def _():
            divide(at)

    for at in range(2):
        staged_copy(0, at).wait()
    for piece in range(max(pieces - 2, 0), pieces):
        partner_copy(piece).wait_send()
        for step in range(1, half):
            peer_copy(step, piece).wait_send()

    pl.loop(0, units)(gather.wait_sends)

    pl.loop(0, flows)(flow.wait_sends)


def finish_kernel(
    parts, ready, done, y_rows, y_cols, gap_rows, gap_cols, out,
    passed, right, chunk_buf, turned, gap_turned, staged,
    right_sem, chunk_sem, read_sem, write_sem, staged_sem
):
    late = chunk_buf.shape[0]
    right_copies = right_loads(parts, y_cols, right, right_sem)
    chunk_copies = [
        chunk_loads(parts, y_rows, ready + index, chunk_buf.at[index], chunk_sem.at[index])
        for index in range(late)
    ]
    rows, tile = staged.shape[1:]
    tiles = right.shape[1] // tile
    part = passed.shape[1]

    def read(index):
        begin = pl.multiple_of(index * part, part)
        return pltpu.make_async_copy(
            done.at[pl.ds(begin, part), :], passed.at[index], read_sem.at[index]
        )

    def write(index):
        begin = pl.multiple_of(index * part, part)
        return pltpu.make_async_copy(
            passed.at[index], out.at[pl.ds(begin, part), :], write_sem.at[index]
        )

    def staged_copy(index, at):
        slot = lax.rem(at, 2)
        span = pl.ds(pl.multiple_of(at * tile, tile), tile)
        return pltpu.make_async_copy(
            staged.at[slot], out.at[pl.ds((ready + index) * rows, rows), span], staged_sem.at[slot]
        )

    for copy in right_copies:
        copy.start()
    for index in range(late):
        for copy in chunk_copies[index]:
            copy.start()

    @pl.loop(0, late * tiles)
    def _(index):
        read(index).start()

    for copy in right_copies:
        copy.wait()
    for index in range(late):
        for copy in chunk_copies[index]:
            copy.wait()
        turn(chunk_buf.at[index], turned, gap_rows, gap_turned, (ready + index) * rows)

        @pl.loop(0, tiles)
        def _(at):
            read(index * tiles + at).wait()
            write(index * tiles + at).start()

            @pl.when(jnp.logical_or(index > 0, at >= 2))
            def _():
                staged_copy(index, at).wait()

            span = pl.ds(pl.multiple_of(at * tile, tile), tile)
            staged[lax.rem(at, 2)] = quotient(turned, right[:, span], gap_turned, gap_cols, span)
            staged_copy(index, at).start()

    for at in range(2):
        staged_copy(0, at).wait()

    @pl.loop(0, late * tiles)
    def _(index):
        write(index).wait()


def update(amplitudes, own, gap_rows, gap_cols, row_count, col_count, collective_id):
    depth, width = own.shape
    rows_width = amplitudes.shape[0]
    pieces = max(1, min(8, depth // 16))
    chunks = max(2, min(CHUNKS, rows_width // 128))
    tile = min(512, width)
    cuts = min(CUTS, width // tile)
    parts = min(SPLIT, pieces)
    late = max(1, chunks * LATE // 8)
    ready = chunks - late
    share = row_count // col_count
    span = rows_width // chunks
    depth_piece, half = depth // pieces, row_count // 2
    bf16, f32, dma = jnp.bfloat16, jnp.float32, pltpu.SemaphoreType.DMA
    scratch = [
        pltpu.VMEM((depth, width), bf16),
        pltpu.VMEM(amplitudes.shape, bf16),
        pltpu.VMEM((pieces, row_count * depth_piece, amplitudes.shape[0]), bf16),
        pltpu.VMEM((half * depth_piece, width), f32),
        pltpu.VMEM((2, depth_piece, width), f32),
        pltpu.VMEM((2, half * depth_piece, width), bf16),
        pltpu.VMEM((pieces, half * depth_piece, width), bf16),
        pltpu.VMEM((2, half - 1, depth_piece, width), bf16),
        pltpu.VMEM((pieces, half - 1, depth_piece, width), bf16),
        pltpu.VMEM((pieces, depth_piece, width), bf16),
        pltpu.VMEM((row_count * depth, span), bf16),
        pltpu.VMEM((span, row_count * depth), bf16),
        pltpu.VMEM((span, 128), f32),
        pltpu.VMEM((2, span, tile), bf16),
        dma((4,)),
        dma((pieces,)),
        dma((pieces,)),
        dma((pieces,)),
        dma((pieces, half)),
        dma((pieces, half)),
        dma((parts * row_count,)),
        dma((parts,)),
        dma((2,)),
    ]
    scratch += spread_sems(row_count, col_count, pieces * cuts, 1)
    scratch += spread_sems(row_count, col_count, parts * chunks, 2)
    scratch += columns_sems(row_count, pieces)
    anywhere = pl.BlockSpec(memory_space=pl.ANY)
    near = pl.BlockSpec(memory_space=pltpu.VMEM)
    _, _, y_rows, y_cols, done = pl.pallas_call(
        functools.partial(dress_kernel, row_count, col_count, pieces, cuts, parts, chunks, ready),
        out_shape=(
            jax.ShapeDtypeStruct((col_count, depth, width), bf16),
            jax.ShapeDtypeStruct((col_count, parts * chunks, share, depth // parts, span), bf16),
            jax.ShapeDtypeStruct((parts * chunks, row_count * depth // parts, span), bf16),
            jax.ShapeDtypeStruct((row_count, depth, width), bf16),
            jax.ShapeDtypeStruct((ready * span, width), bf16),
        ),
        in_specs=[anywhere, anywhere, near, near],
        out_specs=(anywhere,) * 5,
        scratch_shapes=scratch,
        compiler_params=pltpu.CompilerParams(
            collective_id=collective_id, has_side_effects=True, vmem_limit_bytes=67043328
        ),
        name="dress",
    )(amplitudes, own, gap_rows, gap_cols)
    moves = late * (width // tile)
    return pl.pallas_call(
        functools.partial(finish_kernel, parts, ready),
        out_shape=jax.ShapeDtypeStruct(amplitudes.shape, bf16),
        in_specs=[anywhere] * 3 + [near] * 2,
        out_specs=anywhere,
        scratch_shapes=[
            pltpu.VMEM((moves, ready * span // moves, width), bf16),
            pltpu.VMEM((row_count * depth, width), bf16),
            pltpu.VMEM((late, row_count * depth, span), bf16),
            pltpu.VMEM((span, row_count * depth), bf16),
            pltpu.VMEM((span, 128), f32),
            pltpu.VMEM((2, span, tile), bf16),
            dma((parts * row_count,)),
            dma((late, parts)),
            dma((moves,)),
            dma((moves,)),
            dma((2,)),
        ],
        compiler_params=pltpu.CompilerParams(vmem_limit_bytes=67043328),
        name="finish",
    )(done, y_rows, y_cols, gap_rows, gap_cols)


def local(row_count, col_count, amplitudes, cholesky, occ_index, vir_index, eps_occ, eps_vir):
    row_position = lax.axis_index("row")
    col_position = lax.axis_index("col")
    rows_block, cols_block = amplitudes.shape
    gap_rows = pair_gaps(
        occ_index, vir_index, eps_occ, eps_vir, row_position * rows_block, rows_block
    )
    gap_cols = pair_gaps(
        occ_index, vir_index, eps_occ, eps_vir, col_position * cols_block, cols_block
    )
    return update(
        amplitudes, cholesky, gap_rows[None, :], gap_cols[None, :], row_count, col_count, 0
    )


def solution(mesh):
    return jax.shard_map(
        functools.partial(local, mesh.shape["row"], mesh.shape["col"]),
        mesh=mesh,
        in_specs=(
            P(("grp", "row"), "col"),
            P("row", ("grp", "col")),
            P("grp"),
            P("grp"),
            P("grp"),
            P("grp"),
        ),
        out_specs=P(("grp", "row"), "col"),
        check_vma=False,
    )
```

```python
import functools

import jax
import jax.numpy as jnp
from jax import lax
from jax.experimental import pallas as pl
from jax.experimental.pallas import tpu as pltpu
from jax.sharding import PartitionSpec as P

MESH = pl.DeviceIdType.MESH
CUTS = 1
CHUNKS = 8
LATE = 2
SPLIT = 2
PLAIN = 4
PLAIN_CHUNKS = 4
LAUNCH_LEAD = 1
FLOW_LEAD = 2
BEGIN_LEAD = 2
CLOSE_LAG = 1


def picked(index_ref, table):
    wanted = index_ref[...]
    width = 8 if table.shape[0] % 8 == 0 else 1

    def pick(step, total):
        for offset in range(width):
            at = step * width + offset
            total = jnp.where(wanted == at, table[at], total)
        return total

    return lax.fori_loop(0, table.shape[0] // width, pick, jnp.zeros(wanted.shape, jnp.float32))


def enter(row_count, col_count, me_row, me_col):
    barrier = pltpu.get_barrier_semaphore()
    for step in range(1, row_count):
        pl.semaphore_signal(
            barrier,
            inc=1,
            device_id={"row": lax.rem(me_row + step, row_count)},
            device_id_type=MESH,
        )
    for condition, where in ((me_col > 0, -1), (me_col < col_count - 1, 1)):

        @pl.when(condition)
        def _():
            pl.semaphore_signal(
                barrier, inc=1, device_id={"col": me_col + where}, device_id_type=MESH
            )

    neighbours = jnp.minimum(me_col, 1) + jnp.minimum(col_count - 1 - me_col, 1)
    pl.semaphore_wait(barrier, row_count - 1 + neighbours)


class Spread:
    def __init__(self, row_count, col_count, own, rows, held, sems):
        self.row_count, self.col_count = row_count, col_count
        self.own, self.rows, self.held = own, rows, held
        self.send_line, self.recv_line, self.send_row, self.recv_row, self.keep = sems[:5]
        self.send_chain, self.recv_chain = sems[5:]
        self.me_row, self.me_col = lax.axis_index("row"), lax.axis_index("col")
        self.share = row_count // col_count
        home = lax.div(self.me_row, self.share)
        ahead = 1 - 2 * lax.rem(home, 2)
        self.after = self.me_col + ahead
        self.onward = jnp.logical_and(self.after >= 0, self.after < col_count)
        self.distance = (self.me_col - home) * ahead
        self.parts = self.send_chain.shape[1]

    def on(self, side):
        return self.me_col < self.col_count - 1 if side == 0 else self.me_col > 0

    def carried(self, block, side, piece):
        return jnp.logical_or(lax.rem(block + side, 2) == 1, self.plain(piece))

    def source(self, side, hops, piece):
        block = self.me_col - hops if side == 0 else self.me_col + hops
        exists = self.me_col >= hops if side == 0 else self.me_col + hops < self.col_count
        return block, jnp.logical_and(exists, self.carried(block + 2 * hops, side, piece))

    def spread_here(self, block, piece):
        side = jnp.where(block < self.me_col, 0, 1)
        return jnp.logical_or(block == self.me_col, self.carried(block, side, piece))

    def spread(self, block, piece, index, mine=False):
        target = block * self.share + index

        @pl.when(target == self.me_row)
        def _():
            self.keep_copy(block, piece, index, mine).start()

        @pl.when(target != self.me_row)
        def _():
            self.row_copy(block, piece, index, mine).start()

    def begin(self, piece):
        for side in range(2):

            @pl.when(jnp.logical_and(self.on(side), self.carried(self.me_col, side, piece)))
            def _():
                for copy in self.line_copies(side, self.me_col, 0, piece, True):
                    copy.start()

        for index in range(self.share):
            self.spread(self.me_col, piece, index, True)

    def arrive(self, hops, piece):
        for side in range(2):
            block, exists = self.source(side, hops, piece)

            @pl.when(exists)
            def _():
                for copy in self.line_copies(side, block, hops - 1, piece):
                    copy.wait_recv()

                if hops < self.col_count - 1:

                    @pl.when(self.on(side))
                    def _():
                        for copy in self.line_copies(side, block, hops, piece):
                            copy.start()

                for index in range(self.share):
                    self.spread(block, piece, index)

    def line_copies(self, side, block, hops, piece, mine=False):
        return [
            pltpu.make_async_remote_copy(
                src_ref=self.block_ref(block, piece, index, mine),
                dst_ref=self.block_ref(block, piece, index, False),
                send_sem=self.send_line.at[side, hops, piece, index],
                recv_sem=self.recv_line.at[side, hops, piece, index],
                device_id={"col": self.me_col + (1 if side == 0 else -1)},
                device_id_type=MESH,
            )
            for index in range(self.share)
        ]

    def row_copy(self, block, piece, index, mine=False):
        target = block * self.share + index
        return pltpu.make_async_remote_copy(
            src_ref=self.block_ref(block, piece, index, mine),
            dst_ref=self.row_ref(self.me_row, target, piece),
            send_sem=self.send_row.at[block, index, piece],
            recv_sem=self.recv_row.at[self.me_row, piece],
            device_id={"row": target},
            device_id_type=MESH,
        )

    def keep_copy(self, block, piece, index, mine=False):
        return pltpu.make_async_copy(
            self.block_ref(block, piece, index, mine),
            self.row_ref(self.me_row, self.me_row, piece),
            self.keep.at[piece],
        )

    def chain_copy(self, piece, part):
        ref = self.chain_ref(piece, part)
        return pltpu.make_async_remote_copy(
            src_ref=ref,
            dst_ref=ref,
            send_sem=self.send_chain.at[piece, part],
            recv_sem=self.recv_chain.at[piece, part],
            device_id={"col": self.after},
            device_id_type=MESH,
        )

    def wait_rows(self, piece):
        mine = self.row_ref(self.me_row, self.me_row, piece)
        for other in range(self.row_count):

            @pl.when(other != self.me_row)
            def _():
                theirs = self.row_ref(other, self.me_row, piece)
                pltpu.make_async_remote_copy(
                    src_ref=theirs,
                    dst_ref=theirs,
                    send_sem=self.send_row.at[0, 0, piece],
                    recv_sem=self.recv_row.at[other, piece],
                    device_id={"row": other},
                    device_id_type=MESH,
                ).wait_recv()

        pltpu.make_async_copy(mine, mine, self.keep.at[piece]).wait()

    def launch(self, piece):
        @pl.when(self.distance == 0)
        def _():
            self.wait_rows(piece)

            @pl.when(jnp.logical_and(self.onward, jnp.logical_not(self.plain(piece))))
            def _():
                for part in range(self.parts):
                    self.chain_copy(piece, part).start()

    def relay(self, distance, piece):
        @pl.when(jnp.logical_and(self.distance == distance, jnp.logical_not(self.plain(piece))))
        def _():
            for part in range(self.parts):
                self.chain_copy(piece, part).wait_recv()

                @pl.when(self.onward)
                def _():
                    self.chain_copy(piece, part).start()

    def sliced(self, piece):
        plain = jnp.logical_and(self.distance > 0, self.plain(piece))
        return jnp.logical_or(self.distance < 0, plain)

    def settle(self, piece):
        self.relay(self.col_count - 1, piece)

        @pl.when(self.sliced(piece))
        def _():
            self.wait_rows(piece)

    def wait_sends(self, piece):
        for side in range(2):
            for hops in range(self.col_count - 1):
                block, exists = self.source(side, hops, piece)

                @pl.when(jnp.logical_and(exists, self.on(side)))
                def _():
                    for copy in self.line_copies(side, self.me_col, hops, piece):
                        copy.wait_send()

        for block in range(self.col_count):
            for index in range(self.share):

                @pl.when(
                    jnp.logical_and(
                        self.spread_here(block, piece), block * self.share + index != self.me_row
                    )
                )
                def _():
                    self.row_copy(block, piece, index).wait_send()

        chained = jnp.logical_and(self.distance >= 0, jnp.logical_not(self.plain(piece)))

        @pl.when(jnp.logical_and(chained, self.onward))
        def _():
            for part in range(self.parts):
                self.chain_copy(piece, part).wait_send()


class Gather(Spread):
    def __init__(self, row_count, col_count, pieces, cuts, own, rows, held, sems):
        super().__init__(row_count, col_count, own, rows, held, sems)
        self.pieces, self.cuts = pieces, cuts
        self.depth = own.shape[0] // pieces
        self.full = own.shape[1] // self.share
        self.width = self.full // cuts

    def plain(self, unit):
        return unit < self.pieces * self.cuts * PLAIN // 8

    def part(self, piece):
        return pl.ds(pl.multiple_of(piece * self.depth, self.depth), self.depth)

    def span(self, unit, index=0):
        begin = index * self.full + lax.rem(unit, self.cuts) * self.width
        return pl.ds(pl.multiple_of(begin, self.width), self.width)

    def block_ref(self, block, unit, index, mine):
        piece = lax.div(unit, self.cuts)
        if mine:
            return self.own.at[self.part(piece), self.span(unit, index)]
        return self.held.at[block, self.part(piece), self.span(unit, index)]

    def row_ref(self, owner, target, unit):
        half = self.row_count // 2
        other = lax.rem(owner + target, 2)
        base = target + other * (1 - 2 * lax.rem(target, 2))
        slot = lax.div(lax.rem(owner - base + self.row_count, self.row_count), 2) + other * half
        begin = pl.multiple_of(slot * self.depth, self.depth)
        piece = lax.div(unit, self.cuts)
        return self.rows.at[piece, pl.ds(begin, self.depth), self.span(unit)]

    def chain_ref(self, unit, part):
        return self.rows.at[lax.div(unit, self.cuts), :, self.span(unit)]


class Chunks(Spread):
    def __init__(self, row_count, col_count, parts, own, rows, held, sems):
        super().__init__(row_count, col_count, own, rows, held, sems)
        self.chunks = rows.shape[0] // parts
        self.depth = own.shape[0] // parts
        self.width = own.shape[1] // (self.chunks * self.share)

    def plain(self, unit):
        return lax.rem(unit, self.chunks) < self.chunks * PLAIN_CHUNKS // 8

    def block_ref(self, block, unit, index, mine):
        if mine:
            lines = lax.div(unit, self.chunks) * self.depth
            begin = (index * self.chunks + lax.rem(unit, self.chunks)) * self.width
            return self.own.at[
                pl.ds(pl.multiple_of(lines, self.depth), self.depth),
                pl.ds(pl.multiple_of(begin, self.width), self.width),
            ]
        return self.held.at[block, unit, index]

    def row_ref(self, owner, target, unit):
        begin = pl.multiple_of(owner * self.depth, self.depth)
        return self.rows.at[unit, pl.ds(begin, self.depth), :]

    def chain_ref(self, unit, part):
        size = self.rows.shape[1] // self.parts
        return self.rows.at[unit, pl.ds(part * size, size), :]


def spread_sems(row_count, col_count, pieces, parts):
    share = row_count // col_count
    return [
        pltpu.SemaphoreType.DMA((2, col_count, pieces, share)),
        pltpu.SemaphoreType.DMA((2, col_count, pieces, share)),
        pltpu.SemaphoreType.DMA((col_count, share, pieces)),
        pltpu.SemaphoreType.DMA((row_count, pieces)),
        pltpu.SemaphoreType.DMA((pieces,)),
        pltpu.SemaphoreType.DMA((pieces, parts)),
        pltpu.SemaphoreType.DMA((pieces, parts)),
    ]


class Columns:
    def __init__(self, row_count, pieces, own, cols, sems):
        self.row_count, self.pieces, self.own, self.cols = row_count, pieces, own, cols
        self.load, self.send, self.recv, self.send_on = sems
        self.me_row = lax.axis_index("row")
        self.partner = self.me_row + 1 - 2 * lax.rem(self.me_row, 2)
        self.depth = own.shape[0] // pieces

    def part(self, piece):
        return pl.ds(pl.multiple_of(piece * self.depth, self.depth), self.depth)

    def copy(self, owner, target, sem, piece, src=None):
        dst = self.cols.at[owner, self.part(piece), :]
        return pltpu.make_async_remote_copy(
            src_ref=dst if src is None else src,
            dst_ref=dst,
            send_sem=sem,
            recv_sem=self.recv.at[owner, piece],
            device_id={"row": target},
            device_id_type=MESH,
        )

    def peers(self):
        peers = [(0, self.partner)]
        for step in range(1, self.row_count // 2):
            peers.append((step, lax.rem(self.me_row + 2 * step, self.row_count)))
        return peers

    def first(self, slot, target, piece, src):
        return self.copy(self.me_row, target, self.send.at[slot, piece], piece, src)

    def begin(self, piece, src):
        for slot, target in self.peers():
            self.first(slot, target, piece, src).start()

    def arrive(self, piece):
        for slot, owner in self.peers()[1:]:
            self.copy(owner, self.partner, self.send_on.at[slot, piece], piece).wait_recv()
            self.copy(owner, self.partner, self.send_on.at[slot, piece], piece).start()

    def finish(self, piece, src):
        for slot, target in self.peers():
            self.first(slot, target, piece, src).wait_send()
        self.copy(self.partner, self.partner, self.send.at[0, piece], piece).wait_recv()
        for slot, owner in self.peers()[1:]:
            self.copy(owner, self.partner, self.send_on.at[slot, piece], piece).wait_send()
            theirs = lax.rem(self.partner + 2 * slot, self.row_count)
            self.copy(theirs, self.partner, self.send.at[0, piece], piece).wait_recv()


def columns_sems(row_count, pieces):
    return [
        pltpu.SemaphoreType.DMA((pieces,)),
        pltpu.SemaphoreType.DMA((row_count // 2, pieces)),
        pltpu.SemaphoreType.DMA((row_count, pieces)),
        pltpu.SemaphoreType.DMA((row_count // 2, pieces)),
    ]


def right_loads(parts, y_cols, right, sems):
    owners, full, _ = y_cols.shape
    size = full // parts
    return [
        pltpu.make_async_copy(
            y_cols.at[owner, pl.ds(part * size, size), :],
            right.at[pl.ds((part * owners + owner) * size, size), :],
            sems.at[part * owners + owner],
        )
        for part in range(parts)
        for owner in range(owners)
    ]


def chunk_loads(parts, y_rows, index, chunk_ref, sems):
    units, size, _ = y_rows.shape
    return [
        pltpu.make_async_copy(
            y_rows.at[part * (units // parts) + index],
            chunk_ref.at[pl.ds(part * size, size), :],
            sems.at[part],
        )
        for part in range(parts)
    ]


def turn(chunk_ref, turned, gap_rows, gap_turned, index):
    turned[...] = chunk_ref[...].T
    lines = turned.shape[0] // 128
    for line in range(lines):
        gaps = gap_rows[pl.ds(index * lines + line, 1), :]
        gap_turned[pl.ds(line * 128, 128), :] = jnp.broadcast_to(gaps, (128, 128)).T


def quotient(turned, right, gap_turned, gap_cols, at):
    gram = jnp.dot(turned[...], right, preferred_element_type=jnp.float32)
    lines = gram.shape[1] // 128
    gaps = [gap_cols[pl.ds(at * lines + line, 1), :] for line in range(lines)]
    total = jnp.concatenate([gap_turned[...] + line for line in gaps], axis=1)
    return (-gram / total).astype(jnp.bfloat16)


def dress_kernel(
    row_count, col_count, pieces, cuts, parts, chunks, ready, amplitudes, own, occ_index, vir_index, eps_occ, eps_vir,
    held, held_y, y_rows, y_cols, done, gap_rows, gap_cols, dressed, table, rows, mine, kept,
    to_partner, from_partner, to_peer, from_peer, chol, chunk_buf, turned, gap_turned, staged,
    row_indices, col_indices, index_sem, table_sem, chol_sem, partner_send, partner_recv, peer_send, peer_recv,
    right_sem, chunk_sem, staged_sem, *sems
):
    gather = Gather(row_count, col_count, pieces, cuts, own, rows, held, sems[:7])
    full = dressed.shape[0]
    flow = Chunks(row_count, col_count, parts, dressed, y_rows, held_y, sems[7:14])
    columns = Columns(row_count, pieces, dressed, y_cols, sems[14:])
    me_row, depth = gather.me_row, gather.depth
    partner = me_row + 1 - 2 * lax.rem(me_row, 2)
    half = row_count // 2
    split = table_sem.shape[0]
    chunk = table.shape[0] // split
    tile = min(512, table.shape[1])
    tiles = table.shape[1] // tile

    def table_copy(index):
        span = pl.ds(index * chunk, chunk)
        return pltpu.make_async_copy(
            amplitudes.at[span, :], table.at[span, :], table_sem.at[index]
        )

    def chol_copy(piece):
        return pltpu.make_async_copy(
            own.at[gather.part(piece), :], chol.at[piece], chol_sem.at[piece]
        )

    def partner_copy(piece):
        return pltpu.make_async_remote_copy(
            src_ref=to_partner.at[lax.rem(piece, 2)],
            dst_ref=from_partner.at[piece],
            send_sem=partner_send.at[piece],
            recv_sem=partner_recv.at[piece],
            device_id={"row": partner},
            device_id_type=MESH,
        )

    def peer_copy(step, piece):
        return pltpu.make_async_remote_copy(
            src_ref=to_peer.at[lax.rem(piece, 2), step - 1],
            dst_ref=from_peer.at[piece, half - step - 1],
            send_sem=peer_send.at[piece, step],
            recv_sem=peer_recv.at[piece, half - step],
            device_id={"row": lax.rem(me_row + 2 * step, row_count)},
            device_id_type=MESH,
        )

    def multiply(piece, cut):
        @pl.when(jnp.logical_and(cut == 0, piece >= 2))
        def _():
            partner_copy(piece - 2).wait_send()

        @pl.loop(0, tiles // cuts)
        def _(index):
            begin = (cut * (tiles // cuts) + index) * tile
            span = pl.ds(pl.multiple_of(begin, tile), tile)
            product = jnp.dot(
                rows[piece], table[:, span], preferred_element_type=jnp.float32
            )
            mine[:, span] = product[: half * depth]
            to_partner[lax.rem(piece, 2), :, span] = product[half * depth :].astype(jnp.bfloat16)

        @pl.when(cut == cuts - 1)
        def _():
            partner_copy(piece).start()

    def pair(piece):
        partner_copy(piece).wait_recv()

        @pl.when(piece >= 2)
        def _():
            for step in range(1, half):
                peer_copy(step, piece - 2).wait_send()

        @pl.loop(0, tiles)
        def _(index):
            span = pl.ds(pl.multiple_of(index * tile, tile), tile)
            both = mine[:, span] + from_partner[piece, :, span].astype(jnp.float32)
            kept[lax.rem(piece, 2), :, span] = both[:depth]
            for step in range(1, half):
                to_peer[lax.rem(piece, 2), step - 1, :, span] = both[
                    step * depth : (step + 1) * depth
                ].astype(jnp.bfloat16)

        for step in range(1, half):
            peer_copy(step, piece).start()

    def close(piece):
        chol_copy(piece).wait()
        for step in range(1, half):
            peer_copy(step, piece).wait_recv()

        @pl.loop(0, tiles)
        def _(index):
            span = pl.ds(pl.multiple_of(index * tile, tile), tile)
            total = kept[lax.rem(piece, 2), :, span]
            for step in range(1, half):
                total = total + from_peer[piece, step - 1, :, span].astype(jnp.float32)
            total = chol[piece, :, span].astype(jnp.float32) + total
            dressed[gather.part(piece), span] = total.astype(jnp.bfloat16)

    def own_y(piece):
        return dressed.at[gather.part(piece), :]

    def own_cols(piece):
        return pltpu.make_async_copy(
            own_y(piece), y_cols.at[me_row, gather.part(piece), :], columns.load.at[piece]
        )

    def right_copies():
        return right_loads(parts, y_cols, table, right_sem)

    def chunk_copies(index):
        return chunk_loads(parts, y_rows, index, chunk_buf, chunk_sem)

    def staged_copy(index, at):
        slot = lax.rem(at, 2)
        begin = pl.multiple_of(index * flow.width, flow.width)
        span = pl.ds(pl.multiple_of(at * tile, tile), tile)
        return pltpu.make_async_copy(
            staged.at[slot], done.at[pl.ds(begin, flow.width), span], staged_sem.at[slot]
        )

    def divide(index):
        for copy in chunk_copies(index):
            copy.wait()
        turn(chunk_buf, turned, gap_rows, gap_turned, index)

        @pl.loop(0, tiles)
        def _(at):
            @pl.when(jnp.logical_or(index > 0, at >= 2))
            def _():
                staged_copy(index, at).wait()

            span = pl.ds(pl.multiple_of(at * tile, tile), tile)
            right = table[: row_count * full, span]
            staged[lax.rem(at, 2)] = quotient(turned, right, gap_turned, gap_cols, at)
            staged_copy(index, at).start()

    enter(row_count, col_count, gather.me_row, gather.me_col)
    units = pieces * cuts
    per = pieces // parts
    rate = chunks // (per * cuts)
    flow_lead = min(FLOW_LEAD, rate)
    launch_lead = min(LAUNCH_LEAD, units)
    begin_lead = min(BEGIN_LEAD, units)
    pl.loop(0, begin_lead)(gather.begin)
    pairs = ((row_indices, gather.me_row, gap_rows), (col_indices, gather.me_col, gap_cols))

    def index_copies(side):
        indices, block, _ = pairs[side]
        lines = indices.shape[1]
        span = pl.ds(pl.multiple_of(block * lines, lines), lines)
        return [
            pltpu.make_async_copy(source.at[span, :], indices.at[kind], index_sem.at[side, kind])
            for kind, source in enumerate((occ_index, vir_index))
        ]

    for side in range(2):
        for copy in index_copies(side):
            copy.start()
    pl.loop(0, launch_lead)(gather.launch)
    for index in range(split):
        table_copy(index).start()
    for piece in range(pieces):
        chol_copy(piece).start()
    for side in range(2):
        indices, _, gaps = pairs[side]
        for copy in index_copies(side):
            copy.wait()
        gaps[...] = picked(indices.at[1], eps_vir) - picked(indices.at[0], eps_occ)
    multiply_at = cuts + col_count - 2
    pair_at = multiply_at + cuts
    close_at = pair_at + CLOSE_LAG
    arrive_at = close_at + CLOSE_LAG

    def within(at, count, action):
        @pl.when(jnp.logical_and(at >= 0, at < count))
        def _():
            action(at)

    def every(at, count, action):
        @pl.when(jnp.logical_and(lax.rem(at + 8 * cuts * col_count, cuts) == 0, at >= 0))
        def _():
            within(lax.div(at, cuts), count, action)

    def finish_piece(piece):
        close(piece)
        own_cols(piece).start()
        columns.begin(piece, own_y(piece))

        @pl.when(piece == per - 1)
        def _():
            pl.loop(0, flow_lead)(flow.begin)

    lag = jnp.maximum(flow.distance * jnp.where(flow.distance < 0, -1, 1), 2) + 1
    flows = parts * chunks
    flow_at = per * cuts + close_at
    last = (parts - 1) * chunks

    def advance(step):
        for hops in range(1, col_count):
            within(step - hops + 1, flows, functools.partial(flow.arrive, hops))
        for distance in range(1, col_count):
            within(step - distance, flows, functools.partial(flow.relay, distance))
        within(step + flow_lead, flows, flow.begin)
        within(step, flows, flow.launch)
        at = step - lag + 1

        @pl.when(jnp.logical_and(flow.sliced(at), jnp.logical_and(at >= 0, at < flows)))
        def _():
            flow.wait_rows(at)

    @pl.loop(0, pieces * cuts + close_at)
    def _(tick):
        for hops in range(1, col_count):
            within(tick - hops + 1, units, functools.partial(gather.arrive, hops))
        for distance in range(1, col_count - 1):
            within(tick - distance, units, functools.partial(gather.relay, distance))
        within(tick + begin_lead, units, gather.begin)
        within(tick + launch_lead, units, gather.launch)
        within(tick - col_count + 1, units, gather.settle)
        every(tick - pair_at, pieces, pair)
        every(tick - close_at, pieces, finish_piece)

        @pl.when(tick == multiply_at)
        def _():
            for index in range(split):
                table_copy(index).wait()

        within(
            tick - multiply_at,
            units,
            lambda at: multiply(lax.div(at, cuts), lax.rem(at, cuts)),
        )
        every(tick - arrive_at, pieces - 1, columns.arrive)

        @pl.when(tick >= flow_at)
        def _():
            begin = (tick - flow_at) * rate
            pl.loop(begin, begin + rate)(advance)

    @pl.loop(last, flows + col_count)
    def _(step):
        at = step - lag - last
        go = jnp.logical_and(at >= 0, at < ready)

        @pl.when(go)
        def _():
            for copy in chunk_copies(at):
                copy.start()

        advance(step)

        @pl.when(step == last + 2)
        def _():
            columns.arrive(pieces - 1)
            for piece in range(pieces):
                own_cols(piece).wait()
                columns.finish(piece, own_y(piece))
            for copy in right_copies():
                copy.start()
            for copy in right_copies():
                copy.wait()

        @pl.when(go)
        def _():
            divide(at)

    for at in range(2):
        staged_copy(0, at).wait()
    for piece in range(max(pieces - 2, 0), pieces):
        partner_copy(piece).wait_send()
        for step in range(1, half):
            peer_copy(step, piece).wait_send()

    pl.loop(0, units)(gather.wait_sends)

    pl.loop(0, flows)(flow.wait_sends)


def finish_kernel(
    parts, ready, done, y_rows, y_cols, gap_rows, gap_cols, out,
    passed, right, chunk_buf, turned, gap_turned, staged,
    right_sem, chunk_sem, read_sem, write_sem, staged_sem
):
    late = chunk_buf.shape[0]
    right_copies = right_loads(parts, y_cols, right, right_sem)
    chunk_copies = [
        chunk_loads(parts, y_rows, ready + index, chunk_buf.at[index], chunk_sem.at[index])
        for index in range(late)
    ]
    rows, tile = staged.shape[1:]
    tiles = right.shape[1] // tile
    part = passed.shape[1]

    def read(index):
        begin = pl.multiple_of(index * part, part)
        return pltpu.make_async_copy(
            done.at[pl.ds(begin, part), :], passed.at[index], read_sem.at[index]
        )

    def write(index):
        begin = pl.multiple_of(index * part, part)
        return pltpu.make_async_copy(
            passed.at[index], out.at[pl.ds(begin, part), :], write_sem.at[index]
        )

    def staged_copy(index, at):
        slot = lax.rem(at, 2)
        span = pl.ds(pl.multiple_of(at * tile, tile), tile)
        return pltpu.make_async_copy(
            staged.at[slot], out.at[pl.ds((ready + index) * rows, rows), span], staged_sem.at[slot]
        )

    for copy in right_copies:
        copy.start()
    for index in range(late):
        for copy in chunk_copies[index]:
            copy.start()

    @pl.loop(0, late * tiles)
    def _(index):
        read(index).start()

    for copy in right_copies:
        copy.wait()
    for index in range(late):
        for copy in chunk_copies[index]:
            copy.wait()
        turn(chunk_buf.at[index], turned, gap_rows, gap_turned, ready + index)

        @pl.loop(0, tiles)
        def _(at):
            read(index * tiles + at).wait()
            write(index * tiles + at).start()

            @pl.when(jnp.logical_or(index > 0, at >= 2))
            def _():
                staged_copy(index, at).wait()

            span = pl.ds(pl.multiple_of(at * tile, tile), tile)
            staged[lax.rem(at, 2)] = quotient(turned, right[:, span], gap_turned, gap_cols, at)
            staged_copy(index, at).start()

    for at in range(2):
        staged_copy(0, at).wait()

    @pl.loop(0, late * tiles)
    def _(index):
        write(index).wait()


def update(
    amplitudes, own, occ_index, vir_index, eps_occ, eps_vir, row_count, col_count, collective_id
):
    depth, width = own.shape
    rows_width = amplitudes.shape[0]
    pieces = max(1, min(8, depth // 16))
    chunks = max(2, min(CHUNKS, rows_width // 128))
    tile = min(512, width)
    cuts = min(CUTS, width // tile)
    parts = min(SPLIT, pieces)
    late = max(1, chunks * LATE // 8)
    ready = chunks - late
    share = row_count // col_count
    span = rows_width // chunks
    depth_piece, half = depth // pieces, row_count // 2
    bf16, f32, dma = jnp.bfloat16, jnp.float32, pltpu.SemaphoreType.DMA
    scratch = [
        pltpu.VMEM((depth, width), bf16),
        pltpu.VMEM(amplitudes.shape, bf16),
        pltpu.VMEM((pieces, row_count * depth_piece, amplitudes.shape[0]), bf16),
        pltpu.VMEM((half * depth_piece, width), f32),
        pltpu.VMEM((2, depth_piece, width), f32),
        pltpu.VMEM((2, half * depth_piece, width), bf16),
        pltpu.VMEM((pieces, half * depth_piece, width), bf16),
        pltpu.VMEM((2, half - 1, depth_piece, width), bf16),
        pltpu.VMEM((pieces, half - 1, depth_piece, width), bf16),
        pltpu.VMEM((pieces, depth_piece, width), bf16),
        pltpu.VMEM((row_count * depth, span), bf16),
        pltpu.VMEM((span, row_count * depth), bf16),
        pltpu.VMEM((span, 128), f32),
        pltpu.VMEM((2, span, tile), bf16),
        pltpu.VMEM((2, rows_width // 128, 128), jnp.int32),
        pltpu.VMEM((2, width // 128, 128), jnp.int32),
        dma((2, 2)),
        dma((4,)),
        dma((pieces,)),
        dma((pieces,)),
        dma((pieces,)),
        dma((pieces, half)),
        dma((pieces, half)),
        dma((parts * row_count,)),
        dma((parts,)),
        dma((2,)),
    ]
    scratch += spread_sems(row_count, col_count, pieces * cuts, 1)
    scratch += spread_sems(row_count, col_count, parts * chunks, 2)
    scratch += columns_sems(row_count, pieces)
    anywhere = pl.BlockSpec(memory_space=pl.ANY)
    near = pl.BlockSpec(memory_space=pltpu.VMEM)
    table = pl.BlockSpec(memory_space=pltpu.SMEM)
    _, _, y_rows, y_cols, done, gap_rows, gap_cols = pl.pallas_call(
        functools.partial(dress_kernel, row_count, col_count, pieces, cuts, parts, chunks, ready),
        out_shape=(
            jax.ShapeDtypeStruct((col_count, depth, width), bf16),
            jax.ShapeDtypeStruct((col_count, parts * chunks, share, depth // parts, span), bf16),
            jax.ShapeDtypeStruct((parts * chunks, row_count * depth // parts, span), bf16),
            jax.ShapeDtypeStruct((row_count, depth, width), bf16),
            jax.ShapeDtypeStruct((ready * span, width), bf16),
            jax.ShapeDtypeStruct((rows_width // 128, 128), f32),
            jax.ShapeDtypeStruct((width // 128, 128), f32),
        ),
        in_specs=[anywhere] * 4 + [table] * 2,
        out_specs=(anywhere,) * 5 + (near,) * 2,
        scratch_shapes=scratch,
        compiler_params=pltpu.CompilerParams(
            collective_id=collective_id, has_side_effects=True, vmem_limit_bytes=67043328
        ),
        name="dress",
    )(amplitudes, own, occ_index, vir_index, eps_occ, eps_vir)
    moves = late * (width // tile)
    return pl.pallas_call(
        functools.partial(finish_kernel, parts, ready),
        out_shape=jax.ShapeDtypeStruct(amplitudes.shape, bf16),
        in_specs=[anywhere] * 3 + [near] * 2,
        out_specs=anywhere,
        scratch_shapes=[
            pltpu.VMEM((moves, ready * span // moves, width), bf16),
            pltpu.VMEM((row_count * depth, width), bf16),
            pltpu.VMEM((late, row_count * depth, span), bf16),
            pltpu.VMEM((span, row_count * depth), bf16),
            pltpu.VMEM((span, 128), f32),
            pltpu.VMEM((2, span, tile), bf16),
            dma((parts * row_count,)),
            dma((late, parts)),
            dma((moves,)),
            dma((moves,)),
            dma((2,)),
        ],
        compiler_params=pltpu.CompilerParams(vmem_limit_bytes=67043328),
        name="finish",
    )(done, y_rows, y_cols, gap_rows, gap_cols)


def local(row_count, col_count, amplitudes, cholesky, occ_index, vir_index, eps_occ, eps_vir):
    return update(
        amplitudes, cholesky, occ_index.reshape(-1, 128), vir_index.reshape(-1, 128),
        eps_occ, eps_vir, row_count, col_count, 0,
    )


def solution(mesh):
    return jax.shard_map(
        functools.partial(local, mesh.shape["row"], mesh.shape["col"]),
        mesh=mesh,
        in_specs=(
            P(("grp", "row"), "col"),
            P("row", ("grp", "col")),
            P("grp"),
            P("grp"),
            P("grp"),
            P("grp"),
        ),
        out_specs=P(("grp", "row"), "col"),
        check_vma=False,
    )
```

```python
import functools

import jax
import jax.numpy as jnp
from jax import lax
from jax.experimental import pallas as pl
from jax.experimental.pallas import tpu as pltpu
from jax.sharding import PartitionSpec as P

MESH = pl.DeviceIdType.MESH
CUTS = 1
CHUNKS = 8
LATE = 2
SPLIT = 2
PLAIN = 4
PLAIN_CHUNKS = 4
LAUNCH_LEAD = 1
FLOW_LEAD = 2
BEGIN_LEAD = 3
CLOSE_LAG = 1


def picked(index_ref, table):
    wanted = index_ref[...]
    width = 8 if table.shape[0] % 8 == 0 else 1

    def pick(step, total):
        for offset in range(width):
            at = step * width + offset
            total = jnp.where(wanted == at, table[at], total)
        return total

    return lax.fori_loop(0, table.shape[0] // width, pick, jnp.zeros(wanted.shape, jnp.float32))


def enter(row_count, col_count, me_row, me_col):
    barrier = pltpu.get_barrier_semaphore()
    for step in range(1, row_count):
        pl.semaphore_signal(
            barrier,
            inc=1,
            device_id={"row": lax.rem(me_row + step, row_count)},
            device_id_type=MESH,
        )
    for condition, where in ((me_col > 0, -1), (me_col < col_count - 1, 1)):

        @pl.when(condition)
        def _():
            pl.semaphore_signal(
                barrier, inc=1, device_id={"col": me_col + where}, device_id_type=MESH
            )

    neighbours = jnp.minimum(me_col, 1) + jnp.minimum(col_count - 1 - me_col, 1)
    pl.semaphore_wait(barrier, row_count - 1 + neighbours)


class Spread:
    def __init__(self, row_count, col_count, own, rows, held, sems):
        self.row_count, self.col_count = row_count, col_count
        self.own, self.rows, self.held = own, rows, held
        self.send_line, self.recv_line, self.send_row, self.recv_row, self.keep = sems[:5]
        self.send_chain, self.recv_chain = sems[5:]
        self.me_row, self.me_col = lax.axis_index("row"), lax.axis_index("col")
        self.share = row_count // col_count
        home = lax.div(self.me_row, self.share)
        ahead = 1 - 2 * lax.rem(home, 2)
        self.after = self.me_col + ahead
        self.onward = jnp.logical_and(self.after >= 0, self.after < col_count)
        self.distance = (self.me_col - home) * ahead
        self.parts = self.send_chain.shape[1]

    def on(self, side):
        return self.me_col < self.col_count - 1 if side == 0 else self.me_col > 0

    def carried(self, block, side, piece):
        return jnp.logical_or(lax.rem(block + side, 2) == 1, self.plain(piece))

    def source(self, side, hops, piece):
        block = self.me_col - hops if side == 0 else self.me_col + hops
        exists = self.me_col >= hops if side == 0 else self.me_col + hops < self.col_count
        return block, jnp.logical_and(exists, self.carried(block + 2 * hops, side, piece))

    def spread_here(self, block, piece):
        side = jnp.where(block < self.me_col, 0, 1)
        return jnp.logical_or(block == self.me_col, self.carried(block, side, piece))

    def spread(self, block, piece, index, mine=False):
        target = block * self.share + index

        @pl.when(target == self.me_row)
        def _():
            self.keep_copy(block, piece, index, mine).start()

        @pl.when(target != self.me_row)
        def _():
            self.row_copy(block, piece, index, mine).start()

    def begin(self, piece):
        for side in range(2):

            @pl.when(jnp.logical_and(self.on(side), self.carried(self.me_col, side, piece)))
            def _():
                for copy in self.line_copies(side, self.me_col, 0, piece, True):
                    copy.start()

        for index in range(self.share):
            self.spread(self.me_col, piece, index, True)

    def arrive(self, hops, piece):
        for side in range(2):
            block, exists = self.source(side, hops, piece)

            @pl.when(exists)
            def _():
                for copy in self.line_copies(side, block, hops - 1, piece):
                    copy.wait_recv()

                if hops < self.col_count - 1:

                    @pl.when(self.on(side))
                    def _():
                        for copy in self.line_copies(side, block, hops, piece):
                            copy.start()

                for index in range(self.share):
                    self.spread(block, piece, index)

    def line_copies(self, side, block, hops, piece, mine=False):
        return [
            pltpu.make_async_remote_copy(
                src_ref=self.block_ref(block, piece, index, mine),
                dst_ref=self.block_ref(block, piece, index, False),
                send_sem=self.send_line.at[side, hops, piece, index],
                recv_sem=self.recv_line.at[side, hops, piece, index],
                device_id={"col": self.me_col + (1 if side == 0 else -1)},
                device_id_type=MESH,
            )
            for index in range(self.share)
        ]

    def row_copy(self, block, piece, index, mine=False):
        target = block * self.share + index
        return pltpu.make_async_remote_copy(
            src_ref=self.block_ref(block, piece, index, mine),
            dst_ref=self.row_ref(self.me_row, target, piece),
            send_sem=self.send_row.at[block, index, piece],
            recv_sem=self.recv_row.at[self.me_row, piece],
            device_id={"row": target},
            device_id_type=MESH,
        )

    def keep_copy(self, block, piece, index, mine=False):
        return pltpu.make_async_copy(
            self.block_ref(block, piece, index, mine),
            self.row_ref(self.me_row, self.me_row, piece),
            self.keep.at[piece],
        )

    def chain_copy(self, piece, part):
        ref = self.chain_ref(piece, part)
        return pltpu.make_async_remote_copy(
            src_ref=ref,
            dst_ref=ref,
            send_sem=self.send_chain.at[piece, part],
            recv_sem=self.recv_chain.at[piece, part],
            device_id={"col": self.after},
            device_id_type=MESH,
        )

    def wait_rows(self, piece):
        mine = self.row_ref(self.me_row, self.me_row, piece)
        for other in range(self.row_count):

            @pl.when(other != self.me_row)
            def _():
                theirs = self.row_ref(other, self.me_row, piece)
                pltpu.make_async_remote_copy(
                    src_ref=theirs,
                    dst_ref=theirs,
                    send_sem=self.send_row.at[0, 0, piece],
                    recv_sem=self.recv_row.at[other, piece],
                    device_id={"row": other},
                    device_id_type=MESH,
                ).wait_recv()

        pltpu.make_async_copy(mine, mine, self.keep.at[piece]).wait()

    def launch(self, piece):
        @pl.when(self.distance == 0)
        def _():
            self.wait_rows(piece)

            @pl.when(jnp.logical_and(self.onward, jnp.logical_not(self.plain(piece))))
            def _():
                for part in range(self.parts):
                    self.chain_copy(piece, part).start()

    def relay(self, distance, piece):
        @pl.when(jnp.logical_and(self.distance == distance, jnp.logical_not(self.plain(piece))))
        def _():
            for part in range(self.parts):
                self.chain_copy(piece, part).wait_recv()

                @pl.when(self.onward)
                def _():
                    self.chain_copy(piece, part).start()

    def sliced(self, piece):
        plain = jnp.logical_and(self.distance > 0, self.plain(piece))
        return jnp.logical_or(self.distance < 0, plain)

    def settle(self, piece):
        self.relay(self.col_count - 1, piece)

        @pl.when(self.sliced(piece))
        def _():
            self.wait_rows(piece)

    def wait_sends(self, piece):
        for side in range(2):
            for hops in range(self.col_count - 1):
                block, exists = self.source(side, hops, piece)

                @pl.when(jnp.logical_and(exists, self.on(side)))
                def _():
                    for copy in self.line_copies(side, self.me_col, hops, piece):
                        copy.wait_send()

        for block in range(self.col_count):
            for index in range(self.share):

                @pl.when(
                    jnp.logical_and(
                        self.spread_here(block, piece), block * self.share + index != self.me_row
                    )
                )
                def _():
                    self.row_copy(block, piece, index).wait_send()

        chained = jnp.logical_and(self.distance >= 0, jnp.logical_not(self.plain(piece)))

        @pl.when(jnp.logical_and(chained, self.onward))
        def _():
            for part in range(self.parts):
                self.chain_copy(piece, part).wait_send()


class Gather(Spread):
    def __init__(self, row_count, col_count, pieces, cuts, own, rows, held, sems):
        super().__init__(row_count, col_count, own, rows, held, sems)
        self.pieces, self.cuts = pieces, cuts
        self.depth = own.shape[0] // pieces
        self.full = own.shape[1] // self.share
        self.width = self.full // cuts

    def plain(self, unit):
        return unit < self.pieces * self.cuts * PLAIN // 8

    def part(self, piece):
        return pl.ds(pl.multiple_of(piece * self.depth, self.depth), self.depth)

    def span(self, unit, index=0):
        begin = index * self.full + lax.rem(unit, self.cuts) * self.width
        return pl.ds(pl.multiple_of(begin, self.width), self.width)

    def block_ref(self, block, unit, index, mine):
        piece = lax.div(unit, self.cuts)
        if mine:
            return self.own.at[self.part(piece), self.span(unit, index)]
        return self.held.at[block, self.part(piece), self.span(unit, index)]

    def row_ref(self, owner, target, unit):
        half = self.row_count // 2
        other = lax.rem(owner + target, 2)
        base = target + other * (1 - 2 * lax.rem(target, 2))
        slot = lax.div(lax.rem(owner - base + self.row_count, self.row_count), 2) + other * half
        begin = pl.multiple_of(slot * self.depth, self.depth)
        piece = lax.div(unit, self.cuts)
        return self.rows.at[piece, pl.ds(begin, self.depth), self.span(unit)]

    def chain_ref(self, unit, part):
        return self.rows.at[lax.div(unit, self.cuts), :, self.span(unit)]


class Chunks(Spread):
    def __init__(self, row_count, col_count, parts, own, rows, held, sems):
        super().__init__(row_count, col_count, own, rows, held, sems)
        self.chunks = rows.shape[0] // parts
        self.depth = own.shape[0] // parts
        self.width = own.shape[1] // (self.chunks * self.share)

    def plain(self, unit):
        return lax.rem(unit, self.chunks) < self.chunks * PLAIN_CHUNKS // 8

    def block_ref(self, block, unit, index, mine):
        if mine:
            lines = lax.div(unit, self.chunks) * self.depth
            begin = (index * self.chunks + lax.rem(unit, self.chunks)) * self.width
            return self.own.at[
                pl.ds(pl.multiple_of(lines, self.depth), self.depth),
                pl.ds(pl.multiple_of(begin, self.width), self.width),
            ]
        return self.held.at[block, unit, index]

    def row_ref(self, owner, target, unit):
        begin = pl.multiple_of(owner * self.depth, self.depth)
        return self.rows.at[unit, pl.ds(begin, self.depth), :]

    def chain_ref(self, unit, part):
        size = self.rows.shape[1] // self.parts
        return self.rows.at[unit, pl.ds(part * size, size), :]


def spread_sems(row_count, col_count, pieces, parts):
    share = row_count // col_count
    return [
        pltpu.SemaphoreType.DMA((2, col_count, pieces, share)),
        pltpu.SemaphoreType.DMA((2, col_count, pieces, share)),
        pltpu.SemaphoreType.DMA((col_count, share, pieces)),
        pltpu.SemaphoreType.DMA((row_count, pieces)),
        pltpu.SemaphoreType.DMA((pieces,)),
        pltpu.SemaphoreType.DMA((pieces, parts)),
        pltpu.SemaphoreType.DMA((pieces, parts)),
    ]


class Columns:
    def __init__(self, row_count, pieces, own, cols, sems):
        self.row_count, self.pieces, self.own, self.cols = row_count, pieces, own, cols
        self.load, self.send, self.recv, self.send_on = sems
        self.me_row = lax.axis_index("row")
        self.partner = self.me_row + 1 - 2 * lax.rem(self.me_row, 2)
        self.depth = own.shape[0] // pieces

    def part(self, piece):
        return pl.ds(pl.multiple_of(piece * self.depth, self.depth), self.depth)

    def copy(self, owner, target, sem, piece, src=None):
        dst = self.cols.at[owner, self.part(piece), :]
        return pltpu.make_async_remote_copy(
            src_ref=dst if src is None else src,
            dst_ref=dst,
            send_sem=sem,
            recv_sem=self.recv.at[owner, piece],
            device_id={"row": target},
            device_id_type=MESH,
        )

    def peers(self):
        peers = [(0, self.partner)]
        for step in range(1, self.row_count // 2):
            peers.append((step, lax.rem(self.me_row + 2 * step, self.row_count)))
        return peers

    def first(self, slot, target, piece, src):
        return self.copy(self.me_row, target, self.send.at[slot, piece], piece, src)

    def begin(self, piece, src):
        for slot, target in self.peers():
            self.first(slot, target, piece, src).start()

    def arrive(self, piece):
        for slot, owner in self.peers()[1:]:
            self.copy(owner, self.partner, self.send_on.at[slot, piece], piece).wait_recv()
            self.copy(owner, self.partner, self.send_on.at[slot, piece], piece).start()

    def finish(self, piece, src):
        for slot, target in self.peers():
            self.first(slot, target, piece, src).wait_send()
        self.copy(self.partner, self.partner, self.send.at[0, piece], piece).wait_recv()
        for slot, owner in self.peers()[1:]:
            self.copy(owner, self.partner, self.send_on.at[slot, piece], piece).wait_send()
            theirs = lax.rem(self.partner + 2 * slot, self.row_count)
            self.copy(theirs, self.partner, self.send.at[0, piece], piece).wait_recv()


def columns_sems(row_count, pieces):
    return [
        pltpu.SemaphoreType.DMA((pieces,)),
        pltpu.SemaphoreType.DMA((row_count // 2, pieces)),
        pltpu.SemaphoreType.DMA((row_count, pieces)),
        pltpu.SemaphoreType.DMA((row_count // 2, pieces)),
    ]


def right_loads(parts, y_cols, right, sems):
    owners, full, _ = y_cols.shape
    size = full // parts
    return [
        pltpu.make_async_copy(
            y_cols.at[owner, pl.ds(part * size, size), :],
            right.at[pl.ds((part * owners + owner) * size, size), :],
            sems.at[part * owners + owner],
        )
        for part in range(parts)
        for owner in range(owners)
    ]


def chunk_loads(parts, y_rows, index, chunk_ref, sems):
    units, size, _ = y_rows.shape
    return [
        pltpu.make_async_copy(
            y_rows.at[part * (units // parts) + index],
            chunk_ref.at[pl.ds(part * size, size), :],
            sems.at[part],
        )
        for part in range(parts)
    ]


def turn(chunk_ref, turned, gap_rows, gap_turned, index):
    turned[...] = chunk_ref[...].T
    lines = turned.shape[0] // 128
    for line in range(lines):
        gaps = gap_rows[pl.ds(index * lines + line, 1), :]
        gap_turned[pl.ds(line * 128, 128), :] = jnp.broadcast_to(gaps, (128, 128)).T


def quotient(turned, right, gap_turned, gap_cols, at):
    gram = jnp.dot(turned[...], right, preferred_element_type=jnp.float32)
    lines = gram.shape[1] // 128
    gaps = [gap_cols[pl.ds(at * lines + line, 1), :] for line in range(lines)]
    total = jnp.concatenate([gap_turned[...] + line for line in gaps], axis=1)
    return (-gram / total).astype(jnp.bfloat16)


def dress_kernel(
    row_count, col_count, pieces, cuts, parts, chunks, ready, amplitudes, own, occ_index, vir_index, eps_occ, eps_vir,
    held, held_y, y_rows, y_cols, done, gap_rows, gap_cols, dressed, table, rows, mine, kept,
    to_partner, from_partner, to_peer, from_peer, chol, chunk_buf, turned, gap_turned, staged,
    row_indices, col_indices, index_sem, table_sem, chol_sem, partner_send, partner_recv, peer_send, peer_recv,
    right_sem, chunk_sem, staged_sem, *sems
):
    gather = Gather(row_count, col_count, pieces, cuts, own, rows, held, sems[:7])
    full = dressed.shape[0]
    flow = Chunks(row_count, col_count, parts, dressed, y_rows, held_y, sems[7:14])
    columns = Columns(row_count, pieces, dressed, y_cols, sems[14:])
    me_row, depth = gather.me_row, gather.depth
    partner = me_row + 1 - 2 * lax.rem(me_row, 2)
    half = row_count // 2
    split = table_sem.shape[0]
    chunk = table.shape[0] // split
    tile = min(512, table.shape[1])
    tiles = table.shape[1] // tile

    def table_copy(index):
        span = pl.ds(index * chunk, chunk)
        return pltpu.make_async_copy(
            amplitudes.at[span, :], table.at[span, :], table_sem.at[index]
        )

    def chol_copy(piece):
        return pltpu.make_async_copy(
            own.at[gather.part(piece), :], chol.at[piece], chol_sem.at[piece]
        )

    def partner_copy(piece):
        return pltpu.make_async_remote_copy(
            src_ref=to_partner.at[lax.rem(piece, 2)],
            dst_ref=from_partner.at[piece],
            send_sem=partner_send.at[piece],
            recv_sem=partner_recv.at[piece],
            device_id={"row": partner},
            device_id_type=MESH,
        )

    def peer_copy(step, piece):
        return pltpu.make_async_remote_copy(
            src_ref=to_peer.at[lax.rem(piece, 2), step - 1],
            dst_ref=from_peer.at[piece, half - step - 1],
            send_sem=peer_send.at[piece, step],
            recv_sem=peer_recv.at[piece, half - step],
            device_id={"row": lax.rem(me_row + 2 * step, row_count)},
            device_id_type=MESH,
        )

    def multiply(piece, cut):
        @pl.when(jnp.logical_and(cut == 0, piece >= 2))
        def _():
            partner_copy(piece - 2).wait_send()

        @pl.loop(0, tiles // cuts)
        def _(index):
            begin = (cut * (tiles // cuts) + index) * tile
            span = pl.ds(pl.multiple_of(begin, tile), tile)
            product = jnp.dot(
                rows[piece], table[:, span], preferred_element_type=jnp.float32
            )
            mine[:, span] = product[: half * depth]
            to_partner[lax.rem(piece, 2), :, span] = product[half * depth :].astype(jnp.bfloat16)

        @pl.when(cut == cuts - 1)
        def _():
            partner_copy(piece).start()

    def pair(piece):
        partner_copy(piece).wait_recv()

        @pl.when(piece >= 2)
        def _():
            for step in range(1, half):
                peer_copy(step, piece - 2).wait_send()

        @pl.loop(0, tiles)
        def _(index):
            span = pl.ds(pl.multiple_of(index * tile, tile), tile)
            both = mine[:, span] + from_partner[piece, :, span].astype(jnp.float32)
            kept[lax.rem(piece, 2), :, span] = both[:depth]
            for step in range(1, half):
                to_peer[lax.rem(piece, 2), step - 1, :, span] = both[
                    step * depth : (step + 1) * depth
                ].astype(jnp.bfloat16)

        for step in range(1, half):
            peer_copy(step, piece).start()

    def close(piece):
        chol_copy(piece).wait()
        for step in range(1, half):
            peer_copy(step, piece).wait_recv()

        @pl.loop(0, tiles)
        def _(index):
            span = pl.ds(pl.multiple_of(index * tile, tile), tile)
            total = kept[lax.rem(piece, 2), :, span]
            for step in range(1, half):
                total = total + from_peer[piece, step - 1, :, span].astype(jnp.float32)
            total = chol[piece, :, span].astype(jnp.float32) + total
            dressed[gather.part(piece), span] = total.astype(jnp.bfloat16)

    def own_y(piece):
        return dressed.at[gather.part(piece), :]

    def own_cols(piece):
        return pltpu.make_async_copy(
            own_y(piece), y_cols.at[me_row, gather.part(piece), :], columns.load.at[piece]
        )

    def right_copies():
        return right_loads(parts, y_cols, table, right_sem)

    def chunk_copies(index):
        return chunk_loads(parts, y_rows, index, chunk_buf, chunk_sem)

    def staged_copy(index, at):
        slot = lax.rem(at, 2)
        begin = pl.multiple_of(index * flow.width, flow.width)
        span = pl.ds(pl.multiple_of(at * tile, tile), tile)
        return pltpu.make_async_copy(
            staged.at[slot], done.at[pl.ds(begin, flow.width), span], staged_sem.at[slot]
        )

    def divide(index):
        for copy in chunk_copies(index):
            copy.wait()
        turn(chunk_buf, turned, gap_rows, gap_turned, index)

        @pl.loop(0, tiles)
        def _(at):
            @pl.when(jnp.logical_or(index > 0, at >= 2))
            def _():
                staged_copy(index, at).wait()

            span = pl.ds(pl.multiple_of(at * tile, tile), tile)
            right = table[: row_count * full, span]
            staged[lax.rem(at, 2)] = quotient(turned, right, gap_turned, gap_cols, at)
            staged_copy(index, at).start()

    enter(row_count, col_count, gather.me_row, gather.me_col)
    units = pieces * cuts
    per = pieces // parts
    rate = chunks // (per * cuts)
    flow_lead = min(FLOW_LEAD, rate)
    launch_lead = min(LAUNCH_LEAD, units)
    begin_lead = min(BEGIN_LEAD, units)
    pl.loop(0, begin_lead)(gather.begin)
    pairs = ((row_indices, gather.me_row, gap_rows), (col_indices, gather.me_col, gap_cols))

    def index_copies(side):
        indices, block, _ = pairs[side]
        lines = indices.shape[1]
        span = pl.ds(pl.multiple_of(block * lines, lines), lines)
        return [
            pltpu.make_async_copy(source.at[span, :], indices.at[kind], index_sem.at[side, kind])
            for kind, source in enumerate((occ_index, vir_index))
        ]

    for side in range(2):
        for copy in index_copies(side):
            copy.start()
    pl.loop(0, launch_lead)(gather.launch)
    for index in range(split):
        table_copy(index).start()
    for piece in range(pieces):
        chol_copy(piece).start()
    for side in range(2):
        indices, _, gaps = pairs[side]
        for copy in index_copies(side):
            copy.wait()
        gaps[...] = picked(indices.at[1], eps_vir) - picked(indices.at[0], eps_occ)
    multiply_at = cuts + col_count - 2
    pair_at = multiply_at + cuts
    close_at = pair_at + CLOSE_LAG
    arrive_at = close_at + CLOSE_LAG

    def within(at, count, action):
        @pl.when(jnp.logical_and(at >= 0, at < count))
        def _():
            action(at)

    def every(at, count, action):
        @pl.when(jnp.logical_and(lax.rem(at + 8 * cuts * col_count, cuts) == 0, at >= 0))
        def _():
            within(lax.div(at, cuts), count, action)

    def finish_piece(piece):
        close(piece)
        own_cols(piece).start()
        columns.begin(piece, own_y(piece))

        @pl.when(piece == per - 1)
        def _():
            pl.loop(0, flow_lead)(flow.begin)

    lag = jnp.maximum(flow.distance * jnp.where(flow.distance < 0, -1, 1), 2) + 1
    flows = parts * chunks
    flow_at = per * cuts + close_at
    last = (parts - 1) * chunks

    def advance(step):
        for hops in range(1, col_count):
            within(step - hops + 1, flows, functools.partial(flow.arrive, hops))
        for distance in range(1, col_count):
            within(step - distance, flows, functools.partial(flow.relay, distance))
        within(step + flow_lead, flows, flow.begin)
        within(step, flows, flow.launch)
        at = step - lag + 1

        @pl.when(jnp.logical_and(flow.sliced(at), jnp.logical_and(at >= 0, at < flows)))
        def _():
            flow.wait_rows(at)

    @pl.loop(0, pieces * cuts + close_at)
    def _(tick):
        for hops in range(1, col_count):
            within(tick - hops + 1, units, functools.partial(gather.arrive, hops))
        for distance in range(1, col_count - 1):
            within(tick - distance, units, functools.partial(gather.relay, distance))
        within(tick + begin_lead, units, gather.begin)
        within(tick + launch_lead, units, gather.launch)
        within(tick - col_count + 1, units, gather.settle)
        every(tick - pair_at, pieces, pair)
        every(tick - close_at, pieces, finish_piece)

        @pl.when(tick == multiply_at)
        def _():
            for index in range(split):
                table_copy(index).wait()

        within(
            tick - multiply_at,
            units,
            lambda at: multiply(lax.div(at, cuts), lax.rem(at, cuts)),
        )
        every(tick - arrive_at, pieces - 1, columns.arrive)

        @pl.when(tick >= flow_at)
        def _():
            begin = (tick - flow_at) * rate
            pl.loop(begin, begin + rate)(advance)

    @pl.loop(last, flows + col_count)
    def _(step):
        at = step - lag - last
        go = jnp.logical_and(at >= 0, at < ready)

        @pl.when(go)
        def _():
            for copy in chunk_copies(at):
                copy.start()

        advance(step)

        @pl.when(step == last + 2)
        def _():
            columns.arrive(pieces - 1)
            for piece in range(pieces):
                own_cols(piece).wait()
                columns.finish(piece, own_y(piece))
            for copy in right_copies():
                copy.start()
            for copy in right_copies():
                copy.wait()

        @pl.when(go)
        def _():
            divide(at)

    for at in range(2):
        staged_copy(0, at).wait()
    for piece in range(max(pieces - 2, 0), pieces):
        partner_copy(piece).wait_send()
        for step in range(1, half):
            peer_copy(step, piece).wait_send()

    pl.loop(0, units)(gather.wait_sends)

    pl.loop(0, flows)(flow.wait_sends)


def finish_kernel(
    parts, ready, done, y_rows, y_cols, gap_rows, gap_cols, out,
    passed, right, chunk_buf, turned, gap_turned, staged,
    right_sem, chunk_sem, read_sem, write_sem, staged_sem
):
    late = chunk_buf.shape[0]
    right_copies = right_loads(parts, y_cols, right, right_sem)
    chunk_copies = [
        chunk_loads(parts, y_rows, ready + index, chunk_buf.at[index], chunk_sem.at[index])
        for index in range(late)
    ]
    rows, tile = staged.shape[1:]
    tiles = right.shape[1] // tile
    part = passed.shape[1]

    def read(index):
        begin = pl.multiple_of(index * part, part)
        return pltpu.make_async_copy(
            done.at[pl.ds(begin, part), :], passed.at[index], read_sem.at[index]
        )

    def write(index):
        begin = pl.multiple_of(index * part, part)
        return pltpu.make_async_copy(
            passed.at[index], out.at[pl.ds(begin, part), :], write_sem.at[index]
        )

    def staged_copy(index, at):
        slot = lax.rem(at, 2)
        span = pl.ds(pl.multiple_of(at * tile, tile), tile)
        return pltpu.make_async_copy(
            staged.at[slot], out.at[pl.ds((ready + index) * rows, rows), span], staged_sem.at[slot]
        )

    for copy in right_copies:
        copy.start()
    for index in range(late):
        for copy in chunk_copies[index]:
            copy.start()

    @pl.loop(0, late * tiles)
    def _(index):
        read(index).start()

    for copy in right_copies:
        copy.wait()
    for index in range(late):
        for copy in chunk_copies[index]:
            copy.wait()
        turn(chunk_buf.at[index], turned, gap_rows, gap_turned, ready + index)

        @pl.loop(0, tiles)
        def _(at):
            read(index * tiles + at).wait()
            write(index * tiles + at).start()

            @pl.when(jnp.logical_or(index > 0, at >= 2))
            def _():
                staged_copy(index, at).wait()

            span = pl.ds(pl.multiple_of(at * tile, tile), tile)
            staged[lax.rem(at, 2)] = quotient(turned, right[:, span], gap_turned, gap_cols, at)
            staged_copy(index, at).start()

    for at in range(2):
        staged_copy(0, at).wait()

    @pl.loop(0, late * tiles)
    def _(index):
        write(index).wait()


def update(
    amplitudes, own, occ_index, vir_index, eps_occ, eps_vir, row_count, col_count, collective_id
):
    depth, width = own.shape
    rows_width = amplitudes.shape[0]
    pieces = max(1, min(8, depth // 16))
    chunks = max(2, min(CHUNKS, rows_width // 128))
    tile = min(512, width)
    cuts = min(CUTS, width // tile)
    parts = min(SPLIT, pieces)
    late = max(1, chunks * LATE // 8)
    ready = chunks - late
    share = row_count // col_count
    span = rows_width // chunks
    depth_piece, half = depth // pieces, row_count // 2
    bf16, f32, dma = jnp.bfloat16, jnp.float32, pltpu.SemaphoreType.DMA
    scratch = [
        pltpu.VMEM((depth, width), bf16),
        pltpu.VMEM(amplitudes.shape, bf16),
        pltpu.VMEM((pieces, row_count * depth_piece, amplitudes.shape[0]), bf16),
        pltpu.VMEM((half * depth_piece, width), f32),
        pltpu.VMEM((2, depth_piece, width), f32),
        pltpu.VMEM((2, half * depth_piece, width), bf16),
        pltpu.VMEM((pieces, half * depth_piece, width), bf16),
        pltpu.VMEM((2, half - 1, depth_piece, width), bf16),
        pltpu.VMEM((pieces, half - 1, depth_piece, width), bf16),
        pltpu.VMEM((pieces, depth_piece, width), bf16),
        pltpu.VMEM((row_count * depth, span), bf16),
        pltpu.VMEM((span, row_count * depth), bf16),
        pltpu.VMEM((span, 128), f32),
        pltpu.VMEM((2, span, tile), bf16),
        pltpu.VMEM((2, rows_width // 128, 128), jnp.int32),
        pltpu.VMEM((2, width // 128, 128), jnp.int32),
        dma((2, 2)),
        dma((4,)),
        dma((pieces,)),
        dma((pieces,)),
        dma((pieces,)),
        dma((pieces, half)),
        dma((pieces, half)),
        dma((parts * row_count,)),
        dma((parts,)),
        dma((2,)),
    ]
    scratch += spread_sems(row_count, col_count, pieces * cuts, 1)
    scratch += spread_sems(row_count, col_count, parts * chunks, 2)
    scratch += columns_sems(row_count, pieces)
    anywhere = pl.BlockSpec(memory_space=pl.ANY)
    near = pl.BlockSpec(memory_space=pltpu.VMEM)
    table = pl.BlockSpec(memory_space=pltpu.SMEM)
    _, _, y_rows, y_cols, done, gap_rows, gap_cols = pl.pallas_call(
        functools.partial(dress_kernel, row_count, col_count, pieces, cuts, parts, chunks, ready),
        out_shape=(
            jax.ShapeDtypeStruct((col_count, depth, width), bf16),
            jax.ShapeDtypeStruct((col_count, parts * chunks, share, depth // parts, span), bf16),
            jax.ShapeDtypeStruct((parts * chunks, row_count * depth // parts, span), bf16),
            jax.ShapeDtypeStruct((row_count, depth, width), bf16),
            jax.ShapeDtypeStruct((ready * span, width), bf16),
            jax.ShapeDtypeStruct((rows_width // 128, 128), f32),
            jax.ShapeDtypeStruct((width // 128, 128), f32),
        ),
        in_specs=[anywhere] * 4 + [table] * 2,
        out_specs=(anywhere,) * 5 + (near,) * 2,
        scratch_shapes=scratch,
        compiler_params=pltpu.CompilerParams(
            collective_id=collective_id, has_side_effects=True, vmem_limit_bytes=67043328
        ),
        name="dress",
    )(amplitudes, own, occ_index, vir_index, eps_occ, eps_vir)
    moves = late * (width // tile)
    return pl.pallas_call(
        functools.partial(finish_kernel, parts, ready),
        out_shape=jax.ShapeDtypeStruct(amplitudes.shape, bf16),
        in_specs=[anywhere] * 3 + [near] * 2,
        out_specs=anywhere,
        scratch_shapes=[
            pltpu.VMEM((moves, ready * span // moves, width), bf16),
            pltpu.VMEM((row_count * depth, width), bf16),
            pltpu.VMEM((late, row_count * depth, span), bf16),
            pltpu.VMEM((span, row_count * depth), bf16),
            pltpu.VMEM((span, 128), f32),
            pltpu.VMEM((2, span, tile), bf16),
            dma((parts * row_count,)),
            dma((late, parts)),
            dma((moves,)),
            dma((moves,)),
            dma((2,)),
        ],
        compiler_params=pltpu.CompilerParams(vmem_limit_bytes=67043328),
        name="finish",
    )(done, y_rows, y_cols, gap_rows, gap_cols)


def local(row_count, col_count, amplitudes, cholesky, occ_index, vir_index, eps_occ, eps_vir):
    return update(
        amplitudes, cholesky, occ_index.reshape(-1, 128), vir_index.reshape(-1, 128),
        eps_occ, eps_vir, row_count, col_count, 0,
    )


def solution(mesh):
    return jax.shard_map(
        functools.partial(local, mesh.shape["row"], mesh.shape["col"]),
        mesh=mesh,
        in_specs=(
            P(("grp", "row"), "col"),
            P("row", ("grp", "col")),
            P("grp"),
            P("grp"),
            P("grp"),
            P("grp"),
        ),
        out_specs=P(("grp", "row"), "col"),
        check_vma=False,
    )
```
